128 devices in a mesh: row: 8 (over x, y_hi), col: 16 (over y_lo, z, core).
Axes of the slice: x: 4, y: 4 (y_hi: 2, y_lo: 2; y = y_hi * 2 + y_lo), z: 4, core: 2. Of those that a mesh axis runs over, the one named last changes fastest.
Arguments:
- front_trailing: float32 [16384, 16384], P('row', 'col'), may hold values from -6 to 6
- panel_columns: float32 [16384, 1024], P('row', 'col'), may hold values from -0.1875 to 0.1875
- panel_rows: float32 [1024, 16384], P('row', 'col'), may hold values from -6 to 6
- pivots: int32 [1024], replicated, may hold values from 0 to 1023, each once
- diag_inverse: float32 [1024, 1024], replicated, may hold values from -0.1875 to 0.1875
- test_matrix: float32 [16384, 512], P('col'), may hold values from -0.046875 to 0.046875
Outputs:
- schur: float32 [16384, 16384], P('row', 'col')
- off_samples: float32 [16384, 512], P(('row', 'col'))
- leaf_blocks: float32 [16384, 128], P(('row', 'col'))
- group_gram: float32 [8, 512, 512], P('row')
The draws below stay inside these ranges and needn't reach their ends.
Inputs may be any that keep to these rules, and one draw needn't show every extreme that they name: pivots names each of 0 to 1023 once.
All inputs are finite; a program needn't handle non-finite values.
Results may differ from the reference program's by a relative error of at most 0.000084.
Values sent between devices are 32-bit elements; how exact they have to be, the bound alone decides.
A program may use at most 128 MiB of HBM per device.

```python
import jax
import jax.numpy as jnp
from jax import lax

ORDER = 16384
PANEL = 1024
SAMPLES = 512
LEAF = 128
GROUP_ROWS = 4096
N_ROW = 8


def levels(rng, shape, shards, smallest, high):
    level, own = 1.0, jax.random.fold_in(rng, 6)
    for axis_at, blocks in shards:
        steps = jnp.exp(jax.random.uniform(jax.random.fold_in(own, axis_at), (blocks,), jnp.float32, smallest / len(shards), high / len(shards)))
        level = level * jnp.repeat(steps, shape[axis_at] // blocks).reshape([-1 if axis == axis_at else 1 for axis in range(len(shape))])
    return level


def scatter_about(stream_key, dims, spread, reach, pieces=(), kind=jnp.bfloat16):
    drawn = jax.random.normal(stream_key, dims, jnp.float32) * spread
    if len(pieces) > 0:
        drawn = levels(stream_key, dims, pieces, -0.22, 0.18) * drawn
    return jnp.clip(drawn, min=-reach, max=reach).astype(kind)


def setup_inputs(seed: int = 0) -> dict:
    arg_keys = jax.random.split(jax.random.key(seed), 7)
    front_trailing = scatter_about(arg_keys[0], (ORDER, ORDER), 1.0, 6.0, ((0, 8), (1, 16)), jnp.float32)
    panel_columns = scatter_about(arg_keys[1], (ORDER, PANEL), PANEL ** -0.5, 0.1875, ((0, 8), (1, 16)), jnp.float32)
    panel_rows = scatter_about(arg_keys[2], (PANEL, ORDER), 1.0, 6.0, ((0, 8), (1, 16)), jnp.float32)
    pivots = jax.random.permutation(arg_keys[3], PANEL).astype(jnp.int32)
    diag_inverse = scatter_about(arg_keys[4], (PANEL, PANEL), PANEL ** -0.5, 0.1875, (), jnp.float32)
    test_matrix = scatter_about(arg_keys[5], (ORDER, SAMPLES), ORDER ** -0.5, 0.046875, ((0, 16),), jnp.float32)
    return dict(front_trailing=front_trailing, panel_columns=panel_columns, panel_rows=panel_rows, pivots=pivots, diag_inverse=diag_inverse, test_matrix=test_matrix)


def reference(front_trailing, panel_columns, panel_rows, pivots, diag_inverse, test_matrix):
    highest = lax.Precision.HIGHEST
    upper = jnp.take(panel_rows, pivots, axis=0)
    lower = jnp.dot(panel_columns, diag_inverse, precision=highest, preferred_element_type=jnp.float32)
    schur = front_trailing - jnp.dot(lower, upper, precision=highest, preferred_element_type=jnp.float32)
    leaf_ids = jnp.arange(ORDER, dtype=jnp.int32) // LEAF
    masked = jnp.where(leaf_ids[:, None] == leaf_ids[None, :], jnp.zeros_like(schur), schur)
    off_samples = jnp.dot(masked, test_matrix, precision=highest, preferred_element_type=jnp.float32)
    count = ORDER // LEAF
    blocks = jnp.diagonal(schur.reshape(count, LEAF, count, LEAF), axis1=0, axis2=2)
    leaf_blocks = jnp.moveaxis(blocks, -1, 0).reshape(ORDER, LEAF)
    groups = off_samples.reshape(N_ROW // 2, GROUP_ROWS, SAMPLES)
    gram = jnp.einsum("gri,grj->gij", groups, groups, precision=highest) / GROUP_ROWS
    group_gram = jnp.repeat(gram, 2, axis=0)
    return (schur, off_samples, leaf_blocks, group_gram)
```

```python
import jax
import jax.numpy as jnp
from jax import lax
from jax.sharding import PartitionSpec as P

LEAF = 128


def product(left, right):
    return jnp.dot(left, right, precision=lax.Precision.HIGH, preferred_element_type=jnp.float32)


def body(front_trailing, panel_columns, panel_rows, pivots, diag_inverse, test_matrix):
    col_count = lax.axis_size("col")
    row_count = lax.axis_size("row")
    row_index = lax.axis_index("row")
    col_index = lax.axis_index("col")
    height, width = front_trailing.shape
    upper_full = lax.all_gather(panel_rows, "row", axis=0, tiled=True)
    left = lax.all_gather(panel_columns, "col", axis=1, tiled=True)
    upper = jnp.take(upper_full, pivots, axis=0)
    weight = product(diag_inverse, upper)
    schur = front_trailing - product(left, weight)
    rows = row_index * height + jnp.arange(height, dtype=jnp.int32)
    cols = col_index * width + jnp.arange(width, dtype=jnp.int32)
    same_leaf = rows[:, None] // LEAF == cols[None, :] // LEAF
    masked = jnp.where(same_leaf, jnp.zeros_like(schur), schur)
    partial = product(masked, test_matrix)
    count = width // LEAF
    ratio = col_count // row_count
    leaves = height // LEAF
    kept = []
    for leaf in range(leaves):
        held = col_index == row_index * ratio + leaf // count
        block = schur[leaf * LEAF : (leaf + 1) * LEAF, (leaf % count) * LEAF : (leaf % count + 1) * LEAF]
        kept.append(jnp.where(held, block, jnp.zeros_like(block)))
    both = jnp.concatenate([partial, jnp.concatenate(kept, axis=0)], axis=1)
    own = lax.psum_scatter(both, "col", scatter_dimension=0, tiled=True)
    own_samples = own[:, : partial.shape[1]]
    leaf_blocks = own[:, partial.shape[1] :]
    gram = lax.dot_general(
        own_samples,
        own_samples,
        (((0,), (0,)), ((), ())),
        precision=lax.Precision.HIGH,
        preferred_element_type=jnp.float32,
    )
    gram = lax.psum(gram, "col")
    route = [(i, i ^ 1) for i in range(row_count)]
    gram = gram + lax.ppermute(gram, "row", route)
    group_gram = (gram / (2 * height))[None]
    return (schur, own_samples, leaf_blocks, group_gram)


def solution(mesh):
    placed = (P("row", "col"), P("row", "col"), P("row", "col"), P(), P(), P("col", None))
    return jax.shard_map(
        body,
        mesh=mesh,
        in_specs=placed,
        out_specs=(
            P("row", "col"),
            P(("row", "col"), None),
            P(("row", "col"), None),
            P("row", None, None),
        ),
        check_vma=False,
    )
```

```python
import functools

import jax
import jax.numpy as jnp
from jax import lax
from jax.experimental import pallas as pl
from jax.experimental.pallas import tpu as pltpu
from jax.sharding import PartitionSpec as P

LEAF = 128
F32 = jnp.float32
BF16 = jnp.bfloat16
MESH = pl.DeviceIdType.MESH
TILE = 256


def split(x):
    high = x.astype(BF16)
    return high, (x - high.astype(F32)).astype(BF16)


def dot(a, b):
    return jnp.dot(a, b, preferred_element_type=F32)


def dot_nt(a, b):
    return lax.dot_general(a, b, (((1,), (1,)), ((), ())), preferred_element_type=F32)


def dot_tn(a, b):
    return lax.dot_general(a, b, (((0,), (0,)), ((), ())), preferred_element_type=F32)


def at_least(x, k):
    return pl.multiple_of(x, k)


class Sends:
    def __init__(self, sems):
        self.sems, self.made = sems, []

    def start(self, src, dst, recv, device):
        copy = pltpu.make_async_remote_copy(
            src_ref=src, dst_ref=dst, send_sem=self.sems.at[len(self.made)], recv_sem=recv,
            device_id=device, device_id_type=MESH,
        )
        copy.start()
        self.made.append(copy)

    def finish(self):
        for copy in self.made:
            copy.wait_send()


def arrived(dst, recv, send, device):
    pltpu.make_async_remote_copy(
        src_ref=dst, dst_ref=dst, send_sem=send, recv_sem=recv, device_id=device, device_id_type=MESH
    ).wait_recv()


class Gather:
    def __init__(self, sends, recv, source, place, plus, minus, pair):
        self.sends, self.recv, self.source, self.place = sends, recv, source, place
        self.plus, self.minus, self.pair = plus, minus, pair

    def begin(self):
        for piece in range(2):
            self.sends.start(self.source(piece), self.place(0, 0, piece), self.recv.at[piece], self.pair)
        for piece in range(2):
            self.sends.start(self.source(piece), self.place(0, 0, piece), self.recv.at[2 + piece], self.plus)
            self.sends.start(self.source(piece), self.place(0, 0, piece), self.recv.at[4 + piece], self.minus)

    def where(self, slot):
        pair = 1 if slot in (0, 4, 5, 6) else 0
        return {0: 0, 1: -1, 2: 1, 3: 2, 4: -1, 5: 1, 6: 2}[slot], pair

    def wait(self, slot, piece):
        ring, pair = self.where(slot)
        arrived(self.place(ring, pair, piece), self.recv.at[2 * slot + piece], self.sends.sems.at[0], self.plus)

    def spread(self, piece):
        ref = self.place(0, 1, piece)
        self.sends.start(ref, ref, self.recv.at[8 + piece], self.plus)
        self.sends.start(ref, ref, self.recv.at[10 + piece], self.minus)

    def relay(self, pair, piece):
        slot = 6 if pair else 3
        if piece == 0:
            ref = self.place(-1, pair, 0)
            self.sends.start(ref, ref, self.recv.at[2 * slot], self.plus)
        else:
            ref = self.place(1, pair, 1)
            self.sends.start(ref, ref, self.recv.at[2 * slot + 1], self.minus)


def kernel(
    front_hbm, pt_hbm, u_hbm, piv_ref, diag_hbm, test_hbm,
    schur_hbm, off_hbm, leaf_hbm, gram_hbm,
    pt, ug, dhi, dlo, wacc, whi, wlo, uh, ul, fr, t32, thi, tlo, part,
    rc, rz2, rz, ry, gl, gc, ga, go, lb,
    send_sems, p_recv, core_recv, u_recv, rs_send, rc_recv, rz2_recv, rz_recv, ry_recv,
    g_recv, leaf_send, leaf_recv, local, front_sem, out_sem,
):
    row, col = lax.axis_index("row"), lax.axis_index("col")
    x, yh = row // 2, row % 2
    yl, z, core = col // 8, (col % 8) // 2, col % 2
    y = yh * 2 + yl

    def p_col(dz, dy):
        return ((yl + dy) % 2) * 8 + ((z + dz + 4) % 4) * 2 + core

    def u_row(dx, dy):
        return ((x + dx + 4) % 4) * 2 + (yh + dy) % 2

    def plane(q):
        yy, zz = (y + q // 4) % 4, (z + q % 4) % 4
        return yy, zz

    partner = (row, col + 1 - 2 * core)
    z_plus, z_minus = (row, p_col(1, 0)), (row, p_col(-1, 0))
    y_pair = (row, p_col(0, 1))
    x_plus, x_minus = (u_row(1, 0), col), (u_row(-1, 0), col)
    h_pair = (u_row(0, 1), col)

    own_p = at_least(col * 64, 64)
    own_u = at_least(row * 128, 128)
    loads = [
        (diag_hbm, wacc, 0),
        (u_hbm, ug.at[pl.ds(own_u, 128), :], 1),
        (test_hbm, t32, 2),
        (pt_hbm, pt.at[pl.ds(own_p, 64), :], 3),
    ]
    loads = [pltpu.make_async_copy(src, dst, local.at[i]) for src, dst, i in loads]
    for copy in loads:
        copy.start()

    barrier = pltpu.get_barrier_semaphore()
    peers = [x_plus, x_minus]
    for q in range(16):
        yy, zz = plane(q)
        base = (yy % 2) * 8 + zz * 2
        r = x * 2 + yy // 2
        if q:
            peers.append((r, base + core))
        peers.append((r, base + 1 - core))
    for peer in peers:
        pl.semaphore_signal(barrier, inc=1, device_id=peer, device_id_type=MESH)
    pl.semaphore_wait(barrier, len(peers))

    sends = Sends(send_sems)

    def p_place(dz, dy, piece):
        return pt.at[pl.ds(at_least(p_col(dz, dy) * 64, 64), 64), pl.ds(piece * 1024, 1024)]

    def p_other(dz, dy, piece):
        c = p_col(dz, dy) + 1 - 2 * core
        return pt.at[pl.ds(at_least(c * 64, 64), 64), pl.ds(piece * 1024, 1024)]

    def u_place(dx, dy, piece):
        return ug.at[pl.ds(at_least(u_row(dx, dy) * 128 + piece * 64, 64), 64), :]

    pg = Gather(sends, p_recv, lambda i: pt_hbm.at[:, pl.ds(i * 1024, 1024)], p_place, z_plus, z_minus, y_pair)
    us = Gather(sends, u_recv, lambda i: u_hbm.at[pl.ds(i * 64, 64), :], u_place, x_plus, x_minus, h_pair)
    pg.begin()
    us.begin()
    for piece in range(2):
        sends.start(pg.source(piece), p_place(0, 0, piece), core_recv.at[14 + piece], partner)

    def hand(slot, piece):
        ring, pair = pg.where(slot)
        ref = p_place(ring, pair, piece)
        sends.start(ref, ref, core_recv.at[2 * slot + piece], partner)

    def tile_of(i):
        half = i // 4
        j = i % 4
        off = 2 - j + 3 * (j // 2) - 2 * (j // 3)
        return ((yl + 1 - half) % 2) * 4 + (z + off) % 4

    def front_copy(i):
        rows = pl.ds(at_least(tile_of(i) * TILE, TILE), TILE)
        return pltpu.make_async_copy(front_hbm.at[rows, :], fr.at[rows, :], front_sem.at[i])

    for i in range(8):
        front_copy(i).start()

    def one_hot(i, _):
        rows = pl.ds(at_least(i * TILE, TILE), TILE)
        ids = lax.broadcasted_iota(jnp.int32, (TILE, 1024), 0) + i * TILE
        whi[rows, :] = jnp.where(ids == piv_ref[...], 1.0, 0.0).astype(BF16)
        return 0

    lax.fori_loop(0, 4, one_hot, 0)
    loads[0].wait()

    def permute(i, _):
        rows = pl.ds(at_least(i * TILE, TILE), TILE)
        high, low = split(wacc[rows, :])
        dhi[rows, :] = dot_nt(high, whi[...]).astype(BF16)
        dlo[rows, :] = dot_nt(low, whi[...]).astype(BF16)
        return 0

    lax.fori_loop(0, 4, permute, 0)
    for copy in loads[1:]:
        copy.wait()

    def split_test(i, _):
        rows = pl.ds(at_least(i * TILE, TILE), TILE)
        high, low = split(t32[rows, :])
        thi[rows, :] = high
        tlo[rows, :] = low
        return 0

    lax.fori_loop(0, 4, split_test, 0)

    def weight(dx, first=False, last=False):
        start = at_least(((x + dx + 4) % 4) * TILE, TILE)
        high, low = split(ug[pl.ds(start, TILE), :])
        uh[...] = high
        ul[...] = low

        def step(i, _):
            rows = pl.ds(at_least(i * TILE, TILE), TILE)
            dh, dl = dhi[rows, pl.ds(start, TILE)], dlo[rows, pl.ds(start, TILE)]
            total = dot(dh, uh[...]) + dot(dl, uh[...]) + dot(dh, ul[...])
            if not first:
                total = total + wacc[rows, :]
            if last:
                high, low = split(total)
                whi[rows, :] = high
                wlo[rows, :] = low
            else:
                wacc[rows, :] = total
            return 0

        lax.fori_loop(0, 4, step, 0)

    for piece in range(2):
        for slot in (1, 2):
            pg.wait(slot, piece)
        pg.relay(0, piece)
        for slot in (1, 2):
            us.wait(slot, piece)
        us.relay(0, piece)
        for slot in (1, 2):
            hand(slot, piece)
    for piece in range(2):
        pg.wait(0, piece)
        pg.spread(piece)
        hand(0, piece)
    for piece in range(2):
        us.wait(0, piece)
        us.spread(piece)
    weight(0, first=True)
    for piece in range(2):
        pg.wait(3, piece)
        hand(3, piece)
        us.wait(3, piece)
    for piece in range(2):
        for slot in (4, 5):
            pg.wait(slot, piece)
        pg.relay(1, piece)
        for slot in (4, 5):
            us.wait(slot, piece)
        us.relay(1, piece)
        for slot in (4, 5):
            hand(slot, piece)
    weight(-1)
    weight(1)
    for piece in range(2):
        pg.wait(6, piece)
        hand(6, piece)
    for piece in range(2):
        us.wait(6, piece)
    weight(2, last=True)
    for slot in range(8):
        ring, pair = (0, 0) if slot == 7 else pg.where(slot)
        for piece in range(2):
            arrived(p_other(ring, pair, piece), core_recv.at[2 * slot + piece], send_sems.at[0], partner)

    def my_rows(i):
        return pl.ds(at_least(tile_of(i) * TILE + core * 128, 128), 128)

    def its_rows(i):
        return pl.ds(at_least(tile_of(i) * TILE + 128 - core * 128, 128), 128)

    def to_partner(i):
        return pltpu.make_async_remote_copy(
            src_ref=part.at[its_rows(i), :], dst_ref=rc.at[i], send_sem=rs_send.at[i], recv_sem=rc_recv.at[i],
            device_id=partner, device_id_type=MESH,
        )

    def far(i, half, way):
        return pltpu.make_async_remote_copy(
            src_ref=part.at[my_rows(i), pl.ds(way * 256, 256)], dst_ref=rz2.at[way, half],
            send_sem=rs_send.at[8 + 2 * way + half], recv_sem=rz2_recv.at[2 * way + half],
            device_id=z_minus if way else z_plus, device_id_type=MESH,
        )

    def near(i, half, way):
        return pltpu.make_async_remote_copy(
            src_ref=part.at[my_rows(i), :], dst_ref=rz.at[way, half],
            send_sem=rs_send.at[12 + 2 * way + half], recv_sem=rz_recv.at[2 * way + half],
            device_id=z_minus if way else z_plus, device_id_type=MESH,
        )

    def across():
        return pltpu.make_async_remote_copy(
            src_ref=part.at[my_rows(3), :], dst_ref=ry, send_sem=rs_send.at[16], recv_sem=ry_recv.at[0],
            device_id=y_pair, device_id_type=MESH,
        )

    def handle(i):
        half = i // 4
        j = i % 4
        mine = my_rows(i)
        to_partner(i).wait_recv()
        part[mine, :] = part[mine, :] + rc[i]

        @pl.when(j == 0)
        def _():
            far(i, half, 0).start()
            far(i, half, 1).start()

        for way in range(2):
            @pl.when(j == 1 + way)
            def _():
                far(i, half, way).wait_recv()
                lanes = pl.ds(way * 256, 256)
                part[mine, lanes] = part[mine, lanes] + rz2[way, half]
                near(i, half, way).start()

    def gather_line(i, half):
        mine = my_rows(i)
        near(i, half, 0).wait_recv()
        near(i, half, 1).wait_recv()
        part[mine, :] = part[mine, :] + rz[0, half] + rz[1, half]

    def out_copy(i):
        rows = pl.ds(at_least(tile_of(i) * TILE, TILE), TILE)
        return pltpu.make_async_copy(fr.at[rows, :], schur_hbm.at[rows, :], out_sem.at[i])

    def tile(i, _):
        m = tile_of(i)
        rows = pl.ds(at_least(m * TILE, TILE), TILE)
        front_copy(i).wait()
        high, low = split(pt[:, rows].T)
        update = dot(high, whi[...]) + dot(low, whi[...]) + dot(high, wlo[...])
        s = fr[rows, :] - update
        fr[rows, :] = s
        out_copy(i).start()
        row_leaf = row * 16 + m * 2 + lax.broadcasted_iota(jnp.int32, (TILE, 1024), 0) // LEAF
        col_leaf = col * 8 + lax.broadcasted_iota(jnp.int32, (TILE, 1024), 1) // LEAF
        high, low = split(jnp.where(row_leaf == col_leaf, 0.0, s))

        @pl.when(i > 0)
        def _():
            handle(i - 1)

        @pl.when(i == 7)
        def _():
            gather_line(3, 0)
            across().start()

        part[rows, :] = dot(high, thi[...]) + dot(low, thi[...]) + dot(high, tlo[...])
        to_partner(i).start()
        return 0

    lax.fori_loop(0, 8, tile, 0)

    side = col % 2

    def leaf_block(k):
        return fr.at[pl.ds(at_least((side * 8 + k) * LEAF, LEAF), LEAF), pl.ds(k * LEAF, LEAF)]

    def leaf_copy(k):
        return pltpu.make_async_remote_copy(
            src_ref=leaf_block(k), dst_ref=lb, send_sem=leaf_send.at[k], recv_sem=leaf_recv.at[0],
            device_id=(row, side * 8 + k), device_id_type=MESH,
        )

    for k in range(8):
        @pl.when((col // 2 == row) & (side * 8 + k != col))
        def _():
            leaf_copy(k).start()

        @pl.when((col // 2 == row) & (side * 8 + k == col))
        def _():
            pltpu.make_async_copy(leaf_block(k), lb, local.at[4]).start()

    handle(7)
    gather_line(7, 1)
    across().wait_recv()
    mine = my_rows(7)
    samples = part[mine, :] + ry[...]
    part[mine, :] = samples
    off_copy = pltpu.make_async_copy(part.at[mine, :], off_hbm, local.at[5])
    off_copy.start()

    high, low = split(samples)
    gl[...] = dot_tn(high, high) + dot_tn(low, high) + dot_tn(high, low)
    half_rows = pl.ds(at_least(core * 256, 256), 256)
    other_rows = pl.ds(at_least(256 - core * 256, 256), 256)
    sends.start(gl.at[other_rows, :], gc, g_recv.at[0], partner)
    arrived(gc, g_recv.at[0], send_sems.at[0], partner)
    gl[half_rows, :] = gl[half_rows, :] + gc[...]

    def piece(q):
        yy, zz = plane(q)
        device = (x * 2 + yy // 2, (yy % 2) * 8 + zz * 2 + core)
        return pl.ds(at_least(core * 256 + (yy * 4 + zz) * 16, 16), 16), device

    for q in range(1, 16):
        rows, device = piece(q)
        sends.start(gl.at[rows, :], ga.at[q], g_recv.at[q], device)
    total = gl[piece(0)[0], :]
    for q in range(1, 16):
        arrived(ga.at[q], g_recv.at[q], send_sems.at[0], partner)
        total = total + ga[q]
    own_rows = piece(0)[0]
    go[own_rows, :] = total * (1.0 / 4096)
    for q in range(1, 16):
        sends.start(go.at[own_rows, :], go.at[own_rows, :], g_recv.at[15 + q], piece(q)[1])
    for q in range(1, 16):
        rows = piece((4 - q // 4) % 4 * 4 + (4 - q % 4) % 4)[0]
        arrived(go.at[rows, :], g_recv.at[15 + q], send_sems.at[0], partner)
    sends.start(go.at[half_rows, :], go.at[half_rows, :], g_recv.at[31], partner)
    arrived(go.at[other_rows, :], g_recv.at[31], send_sems.at[0], partner)
    gram_copy = pltpu.make_async_copy(go, gram_hbm, local.at[6])
    gram_copy.start()

    holder = row * 2 + col // 8

    @pl.when(holder != col)
    def _():
        leaf_copy(0).wait_recv()

    @pl.when(holder == col)
    def _():
        pltpu.make_async_copy(leaf_block(0), lb, local.at[4]).wait()

    leaf_out = pltpu.make_async_copy(lb, leaf_hbm, local.at[7])
    leaf_out.start()
    for k in range(8):
        @pl.when((col // 2 == row) & (side * 8 + k != col))
        def _():
            leaf_copy(k).wait_send()

    for i in range(8):
        out_copy(i).wait()
        to_partner(i).wait_send()
    for half in range(2):
        for way in range(2):
            far(4 * half, half, way).wait_send()
            near(4 * half + 1 + way, half, way).wait_send()
    across().wait_send()
    sends.finish()
    off_copy.wait()
    gram_copy.wait()
    leaf_out.wait()


def body(front_trailing, panel_columns, panel_rows, pivots, diag_inverse, test_matrix):
    any_space = pl.BlockSpec(memory_space=pl.ANY)
    vmem, dma = pltpu.VMEM, pltpu.SemaphoreType.DMA
    schur, off, leaf, gram = pl.pallas_call(
        kernel,
        out_shape=(
            jax.ShapeDtypeStruct((2048, 1024), F32),
            jax.ShapeDtypeStruct((128, 512), F32),
            jax.ShapeDtypeStruct((128, 128), F32),
            jax.ShapeDtypeStruct((512, 512), F32),
        ),
        in_specs=[any_space, any_space, any_space, pl.BlockSpec(memory_space=pltpu.VMEM), any_space, any_space],
        out_specs=(any_space,) * 4,
        scratch_shapes=[
            vmem((1024, 2048), F32),
            vmem((1024, 1024), F32),
            vmem((1024, 1024), BF16),
            vmem((1024, 1024), BF16),
            vmem((1024, 1024), F32),
            vmem((1024, 1024), BF16),
            vmem((1024, 1024), BF16),
            vmem((TILE, 1024), BF16),
            vmem((TILE, 1024), BF16),
            vmem((2048, 1024), F32),
            vmem((1024, 512), F32),
            vmem((1024, 512), BF16),
            vmem((1024, 512), BF16),
            vmem((2048, 512), F32),
            vmem((8, 128, 512), F32),
            vmem((2, 2, 128, 256), F32),
            vmem((2, 2, 128, 512), F32),
            vmem((128, 512), F32),
            vmem((512, 512), F32),
            vmem((256, 512), F32),
            vmem((16, 16, 512), F32),
            vmem((512, 512), F32),
            vmem((128, 128), F32),
            dma((80,)),
            dma((14,)),
            dma((16,)),
            dma((14,)),
            dma((17,)),
            dma((8,)),
            dma((4,)),
            dma((4,)),
            dma((1,)),
            dma((32,)),
            dma((8,)),
            dma((1,)),
            dma((8,)),
            dma((8,)),
            dma((8,)),
        ],
        compiler_params=pltpu.CompilerParams(
            collective_id=0, has_side_effects=True, vmem_limit_bytes=64_000_000
        ),
        name="front",
    )(front_trailing, panel_columns.T, panel_rows, pivots.reshape(1, -1), diag_inverse, test_matrix)
    return schur, off, leaf, gram[None]


def solution(mesh):
    placed = (P("row", "col"), P("row", "col"), P("row", "col"), P(), P(), P("col", None))
    return jax.shard_map(
        body,
        mesh=mesh,
        in_specs=placed,
        out_specs=(
            P("row", "col"),
            P(("row", "col"), None),
            P(("row", "col"), None),
            P("row", None, None),
        ),
        check_vma=False,
    )
```

```python
import functools

import jax
import jax.numpy as jnp
from jax import lax
from jax.experimental import pallas as pl
from jax.experimental.pallas import tpu as pltpu
from jax.sharding import PartitionSpec as P

LEAF = 128
F32 = jnp.float32
BF16 = jnp.bfloat16
MESH = pl.DeviceIdType.MESH
TILE = 256


def split(x):
    high = x.astype(BF16)
    return high, (x - high.astype(F32)).astype(BF16)


def dot(a, b):
    return jnp.dot(a, b, preferred_element_type=F32)


def dot_nt(a, b):
    return lax.dot_general(a, b, (((1,), (1,)), ((), ())), preferred_element_type=F32)


def dot_tn(a, b):
    return lax.dot_general(a, b, (((0,), (0,)), ((), ())), preferred_element_type=F32)


def at_least(x, k):
    return pl.multiple_of(x, k)


class Sends:
    def __init__(self, sems):
        self.sems, self.made = sems, []

    def start(self, src, dst, recv, device):
        copy = pltpu.make_async_remote_copy(
            src_ref=src, dst_ref=dst, send_sem=self.sems.at[len(self.made)], recv_sem=recv,
            device_id=device, device_id_type=MESH,
        )
        copy.start()
        self.made.append(copy)

    def finish(self):
        for copy in self.made:
            copy.wait_send()


def arrived(dst, recv, send, device):
    pltpu.make_async_remote_copy(
        src_ref=dst, dst_ref=dst, send_sem=send, recv_sem=recv, device_id=device, device_id_type=MESH
    ).wait_recv()


PIECES = 4


class Gather:
    def __init__(self, sends, recv, source, place, plus, minus, pair):
        self.sends, self.recv, self.source, self.place = sends, recv, source, place
        self.plus, self.minus, self.pair = plus, minus, pair

    def begin(self):
        for piece in range(PIECES):
            src, dst = self.source(piece), self.place(0, 0, piece)
            self.sends.start(src, dst, self.recv.at[piece], self.pair)
            self.sends.start(src, dst, self.recv.at[PIECES + piece], self.plus)
            self.sends.start(src, dst, self.recv.at[2 * PIECES + piece], self.minus)

    def where(self, slot):
        return {0: 0, 1: -1, 2: 1, 3: 2, 4: -1, 5: 1, 6: 2, 7: 0}[slot], int(slot in (0, 4, 5, 6))

    def wait(self, slot, *pieces):
        ring, pair = self.where(slot)
        for piece in pieces:
            arrived(
                self.place(ring, pair, piece), self.recv.at[PIECES * slot + piece], self.sends.sems.at[0], self.plus
            )

    def spread(self, *pieces):
        self.wait(0, *pieces)
        for piece in pieces:
            ref = self.place(0, 1, piece)
            self.sends.start(ref, ref, self.recv.at[4 * PIECES + piece], self.plus)
            self.sends.start(ref, ref, self.recv.at[5 * PIECES + piece], self.minus)

    def relay(self, pair, *pieces):
        slot = 6 if pair else 3
        for piece in pieces:
            ring, device = (-1, self.plus) if piece < 2 else (1, self.minus)
            self.wait((1 if ring < 0 else 2) + 3 * pair, piece)
            ref = self.place(ring, pair, piece)
            self.sends.start(ref, ref, self.recv.at[PIECES * slot + piece], device)


def kernel(
    front_hbm, pt_hbm, u_hbm, piv_ref, diag_hbm, test_hbm,
    schur, off, leaf, gram,
    pt, ug, dhi, dlo, wacc, whi, wlo, uh, ul, ph, pl_, fr, thi, tlo, part,
    rc, rz2, rz, ry, sx, gl, ga, gf,
    send_sems, p_recv, core_recv, u_recv, rs_send, rc_recv, rz2_recv, rz_recv, ry_recv,
    g_recv, leaf_send, leaf_recv, local, front_sem,
):
    row, col = lax.axis_index("row"), lax.axis_index("col")
    x, yh = row // 2, row % 2
    yl, z, core = col // 8, (col % 8) // 2, col % 2
    y = yh * 2 + yl

    def p_col(dz, dy):
        return ((yl + dy) % 2) * 8 + ((z + dz + 4) % 4) * 2 + core

    def u_row(dx, dy):
        return ((x + dx + 4) % 4) * 2 + (yh + dy) % 2

    def plane(q):
        yy, zz = (y + q // 4) % 4, (z + q % 4) % 4
        return yy, zz

    partner = (row, col + 1 - 2 * core)
    z_plus, z_minus = (row, p_col(1, 0)), (row, p_col(-1, 0))
    y_pair = (row, p_col(0, 1))
    x_plus, x_minus = (u_row(1, 0), col), (u_row(-1, 0), col)
    h_pair = (u_row(0, 1), col)

    own_p = at_least(col * 64, 64)
    own_u = at_least(yh * 512 + x * 128, 128)
    loads = [
        (diag_hbm, wacc, 0),
        (u_hbm, ug.at[pl.ds(own_u, 128), :], 1),
        (test_hbm, part.at[pl.ds(0, 1024), :], 2),
        (pt_hbm, pt.at[pl.ds(own_p, 64), :], 3),
    ]
    loads = [pltpu.make_async_copy(src, dst, local.at[i]) for src, dst, i in loads]
    for copy in loads:
        copy.start()

    barrier = pltpu.get_barrier_semaphore()
    peers = [x_plus, x_minus, h_pair, y_pair, z_plus, z_minus, partner]
    for peer in peers:
        pl.semaphore_signal(barrier, inc=1, device_id=peer, device_id_type=MESH)
    pl.semaphore_wait(barrier, len(peers))

    sends = Sends(send_sems)

    def p_place(dz, dy, piece):
        return pt.at[pl.ds(at_least(p_col(dz, dy) * 64, 64), 64), pl.ds(piece * 512, 512)]

    def p_other(dz, dy, piece):
        c = p_col(dz, dy) + 1 - 2 * core
        return pt.at[pl.ds(at_least(c * 64, 64), 64), pl.ds(piece * 512, 512)]

    def u_place(dx, dy, piece):
        return ug.at[pl.ds(at_least(((yh + dy) % 2) * 512 + ((x + dx + 4) % 4) * 128 + piece * 32, 32), 32), :]

    pg = Gather(sends, p_recv, lambda i: pt_hbm.at[:, pl.ds(i * 512, 512)], p_place, z_plus, z_minus, y_pair)
    us = Gather(sends, u_recv, lambda i: u_hbm.at[pl.ds(i * 32, 32), :], u_place, x_plus, x_minus, h_pair)
    pg.begin()
    us.begin()
    for piece in range(PIECES):
        sends.start(pg.source(piece), p_place(0, 0, piece), core_recv.at[7 * PIECES + piece], partner)

    def hand(slot, *pieces):
        ring, pair = pg.where(slot)
        for piece in pieces:
            ref = p_place(ring, pair, piece)
            sends.start(ref, ref, core_recv.at[PIECES * slot + piece], partner)

    def tile_of(i):
        half = i // 4
        j = i % 4
        off = 2 - j + 3 * (j // 2) - 2 * (j // 3)
        return ((yl + 1 - half) % 2) * 4 + (z + off) % 4

    def front_copy(i):
        rows = pl.ds(at_least(tile_of(i) * TILE, TILE), TILE)
        return pltpu.make_async_copy(front_hbm.at[rows, :], fr.at[i % 2], front_sem.at[i % 2])

    front_copy(0).start()

    def one_hot(i, _):
        rows = pl.ds(at_least(i * TILE, TILE), TILE)
        k = lax.broadcasted_iota(jnp.int32, (TILE, 1024), 0)
        ids = (i % 2) * 512 + (i // 2) * 128 + k + (k // 128) * 128
        whi[rows, :] = jnp.where(ids == piv_ref[...], 1.0, 0.0).astype(BF16)
        return 0

    lax.fori_loop(0, 4, one_hot, 0)
    loads[0].wait()

    def permute(i, _):
        rows = pl.ds(at_least(i * TILE, TILE), TILE)
        high, low = split(wacc[rows, :])
        dhi[rows, :] = dot_nt(high, whi[...]).astype(BF16)
        dlo[rows, :] = dot_nt(low, whi[...]).astype(BF16)
        return 0

    lax.fori_loop(0, 3, permute, 0)
    pg.relay(0, 0, 1, 2)
    us.relay(0, 0, 1, 2)
    lax.fori_loop(3, 4, permute, 0)
    pg.relay(0, 3)
    us.relay(0, 3)
    pg.spread(0)
    us.spread(0)
    for copy in loads[1:]:
        copy.wait()

    def split_test(i, _):
        rows = pl.ds(at_least(i * TILE, TILE), TILE)
        high, low = split(part[rows, :])
        thi[rows, :] = high
        tlo[rows, :] = low
        return 0

    lax.fori_loop(0, 4, split_test, 0)

    def weight(line, pair, first=False, last=False):
        start = at_least(line * 512 + pair * TILE, TILE)
        high, low = split(ug[pl.ds(start, TILE), :])
        uh[...] = high
        ul[...] = low

        def step(i, _):
            rows = pl.ds(at_least(i * TILE, TILE), TILE)
            dh, dl = dhi[rows, pl.ds(start, TILE)], dlo[rows, pl.ds(start, TILE)]
            total = dot(dh, uh[...]) + dot(dl, uh[...]) + dot(dh, ul[...])
            if not first:
                total = total + wacc[rows, :]
            if last:
                high, low = split(total)
                whi[rows, :] = high
                wlo[rows, :] = low
            else:
                wacc[rows, :] = total
            return 0

        lax.fori_loop(0, 4, step, 0)

    pg.spread(1)
    us.spread(1)
    pg.wait(1, 2, 3)
    pg.wait(2, 0, 1)
    hand(1, 0, 1, 2, 3)
    hand(2, 0, 1, 2, 3)
    hand(0, 0, 1)
    us.wait(1, 2, 3)
    us.wait(2, 0, 1)
    us.wait(3, 0, 1, 2, 3)
    weight(yh, 0, first=True)
    pg.spread(2)
    us.spread(2)
    pg.wait(3, 0, 1, 2, 3)
    hand(3, 0, 1, 2, 3)
    hand(0, 2)
    weight(yh, 1)
    pg.spread(3)
    us.spread(3)
    hand(0, 3)
    pg.relay(1, 0, 1)
    us.relay(1, 0, 1)
    pg.relay(1, 2)
    us.relay(1, 2)
    hand(4, 0, 1)
    pg.wait(5, 0, 1)
    hand(5, 0, 1, 2)
    pg.relay(1, 3)
    us.relay(1, 3)
    pg.wait(4, 2, 3)
    hand(4, 2, 3)
    hand(5, 3)
    us.wait(4, 2, 3)
    us.wait(5, 0, 1)
    weight(1 - yh, x // 2)
    for piece in (0, 2, 1, 3):
        pg.wait(6, piece)
        hand(6, piece)
    us.wait(6, 0, 1, 2, 3)
    weight(1 - yh, 1 - x // 2, last=True)
    for slot in range(8):
        ring, pair = pg.where(slot)
        for piece in range(PIECES):
            arrived(
                p_other(ring, pair, piece), core_recv.at[PIECES * slot + piece], send_sems.at[0], partner
            )

    def my_rows(i):
        return pl.ds(at_least(tile_of(i) * TILE + core * 128, 128), 128)

    def its_rows(i):
        return pl.ds(at_least(tile_of(i) * TILE + 128 - core * 128, 128), 128)

    def to_partner(i):
        return pltpu.make_async_remote_copy(
            src_ref=part.at[its_rows(i), :], dst_ref=rc.at[i], send_sem=rs_send.at[i], recv_sem=rc_recv.at[i],
            device_id=partner, device_id_type=MESH,
        )

    def far(i, half, way):
        return pltpu.make_async_remote_copy(
            src_ref=part.at[my_rows(i), pl.ds(way * 256, 256)], dst_ref=rz2.at[way, half],
            send_sem=rs_send.at[8 + 2 * way + half], recv_sem=rz2_recv.at[2 * way + half],
            device_id=z_minus if way else z_plus, device_id_type=MESH,
        )

    def near(i, half, way):
        return pltpu.make_async_remote_copy(
            src_ref=part.at[my_rows(i), :], dst_ref=rz.at[way, half],
            send_sem=rs_send.at[12 + 2 * way + half], recv_sem=rz_recv.at[2 * way + half],
            device_id=z_minus if way else z_plus, device_id_type=MESH,
        )

    def across():
        return pltpu.make_async_remote_copy(
            src_ref=part.at[my_rows(3), :], dst_ref=ry, send_sem=rs_send.at[16], recv_sem=ry_recv.at[0],
            device_id=y_pair, device_id_type=MESH,
        )

    def handle(i):
        half = i // 4
        j = i % 4
        mine = my_rows(i)
        to_partner(i).wait_recv()
        part[mine, :] = part[mine, :] + rc[i]

        @pl.when(j == 0)
        def _():
            far(i, half, 0).start()
            far(i, half, 1).start()

        for way in range(2):
            @pl.when(j == 1 + way)
            def _():
                far(i, half, way).wait_recv()
                lanes = pl.ds(way * 256, 256)
                part[mine, lanes] = part[mine, lanes] + rz2[way, half]
                near(i, half, way).start()

    def gather_line(i, half):
        mine = my_rows(i)
        near(i, half, 0).wait_recv()
        near(i, half, 1).wait_recv()
        part[mine, :] = part[mine, :] + rz[0, half] + rz[1, half]

    def prepare(i):
        rows = pl.ds(at_least(tile_of(i) * TILE, TILE), TILE)
        high, low = split(pt[:, rows].T)
        ph[i % 2] = high
        pl_[i % 2] = low

    prepare(0)

    def tile(i, _):
        m = tile_of(i)
        rows = pl.ds(at_least(m * TILE, TILE), TILE)
        front_copy(i).wait()

        @pl.when(i < 7)
        def _():
            front_copy(i + 1).start()

        high = ph[i % 2]
        update = dot(high, whi[...]) + dot(pl_[i % 2], whi[...]) + dot(high, wlo[...])
        s = fr[i % 2] - update
        schur[rows, :] = s
        prepare((i + 1) % 8)
        row_leaf = row * 16 + m * 2 + lax.broadcasted_iota(jnp.int32, (TILE, 1024), 0) // LEAF
        col_leaf = col * 8 + lax.broadcasted_iota(jnp.int32, (TILE, 1024), 1) // LEAF
        high, low = split(jnp.where(row_leaf == col_leaf, 0.0, s))

        @pl.when(i > 0)
        def _():
            handle(i - 1)

        @pl.when(i == 7)
        def _():
            gather_line(3, 0)
            across().start()

        part[rows, :] = dot(high, thi[...]) + dot(low, thi[...]) + dot(high, tlo[...])
        to_partner(i).start()
        return 0

    lax.fori_loop(0, 8, tile, 0)

    side = col % 2

    def leaf_block(k):
        return schur.at[pl.ds(at_least((side * 8 + k) * LEAF, LEAF), LEAF), pl.ds(k * LEAF, LEAF)]

    def leaf_copy(k):
        return pltpu.make_async_remote_copy(
            src_ref=leaf_block(k), dst_ref=leaf, send_sem=leaf_send.at[k], recv_sem=leaf_recv.at[0],
            device_id=(row, side * 8 + k), device_id_type=MESH,
        )

    for k in range(8):
        @pl.when((col // 2 == row) & (side * 8 + k != col))
        def _():
            leaf_copy(k).start()

        @pl.when((col // 2 == row) & (side * 8 + k == col))
        def _():
            pltpu.make_async_copy(leaf_block(k), leaf, local.at[4]).start()

    handle(7)
    gather_line(7, 1)
    across().wait_recv()
    mine = my_rows(7)
    samples = part[mine, :] + ry[...]
    off[...] = samples
    sends.start(off, sx, g_recv.at[0], partner)

    uh[:128, :512], ul[:128, :512] = split(samples)
    arrived(sx, g_recv.at[0], send_sems.at[0], partner)
    uh[128:, :512], ul[128:, :512] = split(sx[...])
    for t in range(5):
        i = (1 - core) * (t // 4) + core * (1 + t // 2)
        j = (1 - core) * (t % 4 + t // 4) + core * (2 + t % 2 + t // 4)
        left, right = pl.ds(at_least(i * 128, 128), 128), pl.ds(at_least(j * 128, 128), 128)
        gl[t * 128 : (t + 1) * 128, :] = (
            dot_tn(uh[:, left], uh[:, right]) + dot_tn(ul[:, left], uh[:, right]) + dot_tn(uh[:, left], ul[:, right])
        )

    def chip(q):
        yy, zz = plane(q)
        return yy * 4 + zz, (x * 2 + yy // 2, (yy % 2) * 8 + zz * 2 + core)

    def share(side, q):
        return gf.at[pl.ds(at_least(side * 640 + chip(q)[0] * 40, 8), 40), :]

    for q in range(1, 16):
        index, device = chip(q)
        sends.start(gl.at[pl.ds(at_least(index * 40, 8), 40), :], ga.at[q], g_recv.at[q], device)
    own = chip(0)[0]
    total = gl[pl.ds(at_least(own * 40, 8), 40), :]
    for q in range(1, 16):
        arrived(ga.at[q], g_recv.at[q], send_sems.at[0], partner)
        total = total + ga[q]
    gf[pl.ds(at_least(core * 640 + own * 40, 8), 40), :] = total * (1.0 / 4096)
    for q in range(1, 16):
        sends.start(share(core, 0), share(core, 0), g_recv.at[15 + q], chip(q)[1])
    sends.start(share(core, 0), share(core, 0), g_recv.at[31], partner)
    for q in range(1, 16):
        back = (4 - q // 4) % 4 * 4 + (4 - q % 4) % 4
        arrived(share(core, back), g_recv.at[15 + q], send_sems.at[0], partner)
        sends.start(share(core, back), share(core, back), g_recv.at[31 + q], partner)
    for q in range(16):
        back = (4 - q // 4) % 4 * 4 + (4 - q % 4) % 4
        arrived(share(1 - core, back), g_recv.at[31 + q], send_sems.at[0], partner)
    blocks = ((0, 0), (0, 1), (0, 2), (0, 3), (1, 1), (1, 2), (1, 3), (2, 2), (2, 3), (3, 3))
    for b, (i, j) in enumerate(blocks):
        block = gf[b * 128 : (b + 1) * 128, :]
        gram[i * 128 : (i + 1) * 128, j * 128 : (j + 1) * 128] = block
        if i != j:
            gram[j * 128 : (j + 1) * 128, i * 128 : (i + 1) * 128] = block.T

    holder = row * 2 + col // 8

    @pl.when(holder != col)
    def _():
        leaf_copy(0).wait_recv()

    @pl.when(holder == col)
    def _():
        pltpu.make_async_copy(leaf_block(0), leaf, local.at[4]).wait()

    for k in range(8):
        @pl.when((col // 2 == row) & (side * 8 + k != col))
        def _():
            leaf_copy(k).wait_send()

    for i in range(8):
        to_partner(i).wait_send()
    for half in range(2):
        for way in range(2):
            far(4 * half, half, way).wait_send()
            near(4 * half + 1 + way, half, way).wait_send()
    across().wait_send()
    sends.finish()


def emit(*refs):
    copies = [pltpu.make_async_copy(refs[i], refs[4 + i], refs[8].at[i]) for i in range(4)]
    for copy in copies:
        copy.start()
    for copy in copies:
        copy.wait()


def body(front_trailing, panel_columns, panel_rows, pivots, diag_inverse, test_matrix):
    hbm = pl.BlockSpec(memory_space=pltpu.HBM)
    vmem, dma = pltpu.VMEM, pltpu.SemaphoreType.DMA
    schur, off, leaf, gram = pl.pallas_call(
        kernel,
        out_shape=(
            pltpu.VMEM((2048, 1024), F32),
            pltpu.VMEM((128, 512), F32),
            pltpu.VMEM((128, 128), F32),
            pltpu.VMEM((512, 512), F32),
        ),
        in_specs=[hbm, hbm, hbm, pl.BlockSpec(memory_space=pltpu.VMEM), hbm, hbm],
        out_specs=(pl.BlockSpec(memory_space=pltpu.VMEM),) * 4,
        scratch_shapes=[
            vmem((1024, 2048), F32),
            vmem((1024, 1024), F32),
            vmem((1024, 1024), BF16),
            vmem((1024, 1024), BF16),
            vmem((1024, 1024), F32),
            vmem((1024, 1024), BF16),
            vmem((1024, 1024), BF16),
            vmem((TILE, 1024), BF16),
            vmem((TILE, 1024), BF16),
            vmem((2, TILE, 1024), BF16),
            vmem((2, TILE, 1024), BF16),
            vmem((2, TILE, 1024), F32),
            vmem((1024, 512), BF16),
            vmem((1024, 512), BF16),
            vmem((2048, 512), F32),
            vmem((8, 128, 512), F32),
            vmem((2, 2, 128, 256), F32),
            vmem((2, 2, 128, 512), F32),
            vmem((128, 512), F32),
            vmem((128, 512), F32),
            vmem((640, 128), F32),
            vmem((16, 40, 128), F32),
            vmem((1280, 128), F32),
            dma((160,)),
            dma((7 * PIECES,)),
            dma((8 * PIECES,)),
            dma((7 * PIECES,)),
            dma((17,)),
            dma((8,)),
            dma((4,)),
            dma((4,)),
            dma((1,)),
            dma((48,)),
            dma((8,)),
            dma((1,)),
            dma((5,)),
            dma((2,)),
        ],
        compiler_params=pltpu.CompilerParams(
            collective_id=0, has_side_effects=True, vmem_limit_bytes=49_000_000
        ),
        name="front",
    )(*[pltpu.with_memory_space_constraint(a, pltpu.HBM) for a in (front_trailing, panel_columns.T, panel_rows)],
      pivots.reshape(1, -1), *[pltpu.with_memory_space_constraint(a, pltpu.HBM) for a in (diag_inverse, test_matrix)])
    schur, off, leaf, gram = pl.pallas_call(
        emit,
        out_shape=[jax.ShapeDtypeStruct(a.shape, F32) for a in (schur, off, leaf, gram)],
        in_specs=[pl.BlockSpec(memory_space=pltpu.VMEM)] * 4,
        out_specs=[hbm] * 4,
        scratch_shapes=[dma((4,))],
        compiler_params=pltpu.CompilerParams(vmem_limit_bytes=2_000_000),
        name="emit",
    )(schur, off, leaf, gram)
    return schur, off, leaf, gram[None]


def solution(mesh):
    placed = (P("row", "col"), P("row", "col"), P("row", "col"), P(), P(), P("col", None))
    return jax.shard_map(
        body,
        mesh=mesh,
        in_specs=placed,
        out_specs=(
            P("row", "col"),
            P(("row", "col"), None),
            P(("row", "col"), None),
            P("row", None, None),
        ),
        check_vma=False,
    )
```

```python
import functools

import jax
import jax.numpy as jnp
from jax import lax
from jax.experimental import pallas as pl
from jax.experimental.pallas import tpu as pltpu
from jax.sharding import PartitionSpec as P

LEAF = 128
F32 = jnp.float32
BF16 = jnp.bfloat16
MESH = pl.DeviceIdType.MESH
TILE = 256


def split(x):
    high = x.astype(BF16)
    return high, (x - high.astype(F32)).astype(BF16)


def dot(a, b):
    return jnp.dot(a, b, preferred_element_type=F32)


def dot_nt(a, b):
    return lax.dot_general(a, b, (((1,), (1,)), ((), ())), preferred_element_type=F32)


def dot_tn(a, b):
    return lax.dot_general(a, b, (((0,), (0,)), ((), ())), preferred_element_type=F32)


def at_least(x, k):
    return pl.multiple_of(x, k)


class Sends:
    def __init__(self, sem):
        self.sem, self.count = sem, 0

    def start(self, src, dst, recv, device):
        self.count += 1
        pltpu.make_async_remote_copy(
            src_ref=src, dst_ref=dst, send_sem=self.sem, recv_sem=recv, device_id=device, device_id_type=MESH
        ).start()

    def finish(self, whole):
        pltpu.make_async_copy(whole, whole, self.sem).wait()


def arrived(dst, recv):
    pltpu.make_async_copy(dst, dst, recv).wait()


PIECES = 4


class Gather:
    def __init__(self, sends, recv, source, place, plus, minus, pair):
        self.sends, self.recv, self.source, self.place = sends, recv, source, place
        self.plus, self.minus, self.pair = plus, minus, pair

    def to_pair(self, piece):
        self.sends.start(self.source(piece), self.place(0, 0, piece), self.recv.at[piece], self.pair)

    def own(self, piece):
        src, dst = self.source(piece), self.place(0, 0, piece)
        self.sends.start(src, dst, self.recv.at[PIECES + piece], self.plus)
        self.sends.start(src, dst, self.recv.at[2 * PIECES + piece], self.minus)

    def where(self, slot):
        return {0: 0, 1: -1, 2: 1, 3: 2, 4: -1, 5: 1, 6: 2, 7: 0}[slot], int(slot in (0, 4, 5, 6))

    def wait(self, slot, *pieces):
        ring, pair = self.where(slot)
        for piece in pieces:
            arrived(self.place(ring, pair, piece), self.recv.at[PIECES * slot + piece])

    def spread(self, piece, up=True, down=True):
        ref = self.place(0, 1, piece)
        if up:
            self.sends.start(ref, ref, self.recv.at[4 * PIECES + piece], self.plus)
        if down:
            self.sends.start(ref, ref, self.recv.at[5 * PIECES + piece], self.minus)

    def relay(self, pair, piece):
        ring, device = (1, self.minus) if piece % 2 else (-1, self.plus)
        self.wait((1 if ring < 0 else 2) + 3 * pair, piece)
        ref = self.place(ring, pair, piece)
        self.sends.start(ref, ref, self.recv.at[PIECES * (6 if pair else 3) + piece], device)


def kernel(
    front_hbm, pt_hbm, u_hbm, piv_ref, diag_hbm, test_hbm,
    schur, off, leaf, gram,
    pt, ug, dhi, dlo, wacc, whi, wlo, uh, ul, ph, pl_, fr, thi, tlo, part,
    rc, rz2, rz, ry, sx, gl, ga, gf,
    send_sems, p_recv, core_recv, u_recv, rs_send, rc_recv, rz2_recv, rz_recv, ry_recv,
    g_recv, leaf_send, leaf_recv, local, front_sem,
):
    row, col = lax.axis_index("row"), lax.axis_index("col")
    x, yh = row // 2, row % 2
    yl, z, core = col // 8, (col % 8) // 2, col % 2
    y = yh * 2 + yl

    def p_col(dz, dy):
        return ((yl + dy) % 2) * 8 + ((z + dz + 4) % 4) * 2 + core

    def u_row(dx, dy):
        return ((x + dx + 4) % 4) * 2 + (yh + dy) % 2

    def plane(q):
        yy, zz = (y + q // 4) % 4, (z + q % 4) % 4
        return yy, zz

    partner = (row, col + 1 - 2 * core)
    z_plus, z_minus = (row, p_col(1, 0)), (row, p_col(-1, 0))
    y_pair = (row, p_col(0, 1))
    x_plus, x_minus = (u_row(1, 0), col), (u_row(-1, 0), col)
    h_pair = (u_row(0, 1), col)

    own_p = at_least(col * 64, 64)
    own_u = at_least(yh * 512 + x * 128, 128)
    loads = [
        (diag_hbm, wacc, 0),
        (u_hbm, ug.at[pl.ds(own_u, 128), :], 1),
        (test_hbm, part.at[pl.ds(0, 1024), :], 2),
        (pt_hbm, pt.at[pl.ds(own_p, 64), :], 3),
    ]
    loads = [pltpu.make_async_copy(src, dst, local.at[i]) for src, dst, i in loads]
    for copy in loads:
        copy.start()

    barrier = pltpu.get_barrier_semaphore()
    peers = [x_plus, x_minus, h_pair, y_pair, z_plus, z_minus, partner]
    for peer in peers:
        pl.semaphore_signal(barrier, inc=1, device_id=peer, device_id_type=MESH)
    pl.semaphore_wait(barrier, len(peers))

    p_sends, u_sends = Sends(send_sems.at[0]), Sends(send_sems.at[1])

    def p_place(dz, dy, piece):
        return pt.at[pl.ds(at_least(p_col(dz, dy) * 64, 64), 64), pl.ds(piece * 512, 512)]

    def u_place(dx, dy, piece):
        rows = pl.ds(at_least(((yh + dy) % 2) * 512 + ((x + dx + 4) % 4) * 128, 128), 128)
        return ug.at[rows, pl.ds(piece * 256, 256)]

    pg = Gather(p_sends, p_recv, lambda i: pt_hbm.at[:, pl.ds(i * 512, 512)], p_place, z_plus, z_minus, y_pair)
    us = Gather(u_sends, u_recv, lambda i: u_hbm.at[:, pl.ds(i * 256, 256)], u_place, x_plus, x_minus, h_pair)
    both = (pg, us)
    for piece in range(PIECES):
        for g in both:
            g.to_pair(piece)
    for piece in range(2):
        for g in both:
            g.own(piece)
    for piece in range(PIECES):
        p_sends.start(pg.source(piece), p_place(0, 0, piece), core_recv.at[piece // 2], partner)

    def hand(slot, *pieces):
        ring, pair = pg.where(slot)
        for piece in pieces:
            ref = p_place(ring, pair, piece)
            p_sends.start(ref, ref, core_recv.at[piece // 2], partner)

    def tile_of(i):
        half = i % 2
        j = i // 2
        off = 2 - j + 3 * (j // 2) - 2 * (j // 3)
        return ((yl + 1 - half) % 2) * 4 + (z + off) % 4

    def front_copy(i):
        rows = pl.ds(at_least(tile_of(i) * TILE, TILE), TILE)
        return pltpu.make_async_copy(front_hbm.at[rows, :], fr.at[i % 2], front_sem.at[i % 2])

    def early_front(m):
        lanes = pl.ds(0, 512)
        return pltpu.make_async_copy(
            front_hbm.at[pl.ds(m * TILE, TILE), lanes], fr.at[m % 2, :, lanes], front_sem.at[m % 2]
        )

    early_front(0).start()
    early_front(1).start()

    def one_hot(i, _):
        rows = pl.ds(at_least(i * TILE, TILE), TILE)
        k = lax.broadcasted_iota(jnp.int32, (TILE, 1024), 0)
        ids = (i % 2) * 512 + (i // 2) * 128 + k + (k // 128) * 128
        whi[rows, :] = jnp.where(ids == piv_ref[...], 1.0, 0.0).astype(BF16)
        return 0

    lax.fori_loop(0, 4, one_hot, 0)
    loads[0].wait()

    def permute(i, _):
        rows = pl.ds(at_least(i * TILE, TILE), TILE)
        high, low = split(wacc[rows, :])
        dhi[rows, :] = dot_nt(high, whi[...]).astype(BF16)
        dlo[rows, :] = dot_nt(low, whi[...]).astype(BF16)
        return 0

    lax.fori_loop(0, 2, permute, 0)
    for g in both:
        g.relay(0, 0)
        g.relay(0, 1)
    for g in both:
        g.wait(0, 0)
        g.spread(0)
        g.own(2)
    lax.fori_loop(2, 4, permute, 0)
    for copy in loads[1:]:
        copy.wait()

    def split_test(i, _):
        rows = pl.ds(at_least(i * TILE, TILE), TILE)
        high, low = split(part[rows, :])
        thi[rows, :] = high
        tlo[rows, :] = low
        return 0

    lax.fori_loop(0, 4, split_test, 0)

    def weight(line, pair, half, first=False, last=False):
        start = at_least(line * 512 + pair * TILE, TILE)
        lanes = slice(half * 512, half * 512 + 512)
        uh[:, :512], ul[:, :512] = split(ug[pl.ds(start, TILE), lanes])

        def step(i, _):
            rows = pl.ds(at_least(i * TILE, TILE), TILE)
            dh, dl = dhi[rows, pl.ds(start, TILE)], dlo[rows, pl.ds(start, TILE)]
            total = dot(dh, uh[:, :512]) + dot(dl, uh[:, :512]) + dot(dh, ul[:, :512])
            if not first:
                total = total + wacc[rows, lanes]
            if last:
                whi[rows, lanes], wlo[rows, lanes] = split(total)
            else:
                wacc[rows, lanes] = total
            return 0

        lax.fori_loop(0, 4, step, 0)

    def from_partner(which):
        arrived(pt.at[pl.ds(0, 256), :], core_recv.at[which])

    def prepare(m, slot):
        rows = pl.ds(at_least(m * TILE, TILE), TILE)
        ph[slot], pl_[slot] = split(pt[:, rows].T)

    def half_tile(m, slot, half, ahead=None, between=None):
        rows = pl.ds(at_least(m * TILE, TILE), TILE)
        lanes = slice(half * 512, half * 512 + 512)
        high = ph[slot]
        update = dot(high, whi[:, lanes]) + dot(pl_[slot], whi[:, lanes]) + dot(high, wlo[:, lanes])
        if ahead is not None:
            ahead()
        s = fr[slot, :, lanes] - update
        schur[rows, lanes] = s
        row_leaf = row * 16 + m * 2 + lax.broadcasted_iota(jnp.int32, (TILE, 512), 0) // LEAF
        col_leaf = col * 8 + half * 4 + lax.broadcasted_iota(jnp.int32, (TILE, 512), 1) // LEAF
        high, low = split(jnp.where(row_leaf == col_leaf, 0.0, s))
        if between is not None:
            between()
        samples = dot(high, thi[lanes, :]) + dot(low, thi[lanes, :]) + dot(high, tlo[lanes, :])
        part[rows, :] = part[rows, :] + samples if half else samples

    def early(m):
        early_front(m).wait()
        if m == 0:
            prepare(0, 0)
        half_tile(m, m % 2, 0, None if m == 3 else lambda: prepare(m + 1, (m + 1) % 2))
        if m < 2:
            early_front(m + 2).start()

    pg.wait(1, 1)
    pg.wait(2, 0)
    hand(1, 0, 1)
    hand(2, 0, 1)
    hand(0, 0)
    us.wait(1, 1)
    us.wait(2, 0)
    pg.wait(3, 0, 1)
    hand(3, 0, 1)
    us.wait(3, 0, 1)
    for g in both:
        g.wait(0, 1)
        g.spread(1)
    hand(0, 1)
    weight(yh, 0, 0, first=True)
    for g in both:
        g.relay(1, 0)
        g.own(3)
    hand(4, 0)
    weight(yh, 1, 0)
    for g in both:
        g.relay(1, 1)
        g.relay(0, 2)
        g.wait(0, 2)
        g.spread(2)
    pg.wait(5, 0)
    pg.wait(4, 1)
    hand(5, 0, 1)
    hand(4, 1)
    us.wait(5, 0)
    us.wait(4, 1)
    weight(1 - yh, x // 2, 0)
    for g in both:
        g.relay(0, 3)
    hand(0, 2)
    pg.wait(6, 0, 1)
    hand(6, 0, 1)
    us.wait(6, 0, 1)
    weight(1 - yh, 1 - x // 2, 0, last=True)
    from_partner(0)
    early(0)
    for g in both:
        g.wait(0, 3)
        g.spread(3)
    hand(0, 3)
    pg.wait(1, 3)
    pg.wait(2, 2)
    hand(1, 2, 3)
    hand(2, 2, 3)
    us.wait(1, 3)
    us.wait(2, 2)
    early(1)
    for g in both:
        g.relay(1, 2)
    hand(4, 2)
    pg.wait(3, 2, 3)
    hand(3, 2, 3)
    us.wait(3, 2, 3)
    early(2)
    weight(yh, 0, 1, first=True)
    for g in both:
        g.relay(1, 3)
    hand(5, 3)
    early(3)
    front_copy(0).start()
    weight(yh, 1, 1)
    pg.wait(4, 3)
    pg.wait(5, 2)
    hand(4, 3)
    hand(5, 2)
    us.wait(4, 3)
    us.wait(5, 2)
    weight(1 - yh, x // 2, 1)
    pg.wait(6, 2, 3)
    hand(6, 2, 3)
    us.wait(6, 2, 3)
    weight(1 - yh, 1 - x // 2, 1, last=True)
    from_partner(1)

    def my_rows(i):
        return pl.ds(at_least(tile_of(i) * TILE + core * 128, 128), 128)

    def its_rows(i):
        return pl.ds(at_least(tile_of(i) * TILE + 128 - core * 128, 128), 128)

    def to_partner(i):
        return pltpu.make_async_remote_copy(
            src_ref=part.at[its_rows(i), :], dst_ref=rc.at[i], send_sem=rs_send.at[i], recv_sem=rc_recv.at[i],
            device_id=partner, device_id_type=MESH,
        )

    def far(i, half, way):
        return pltpu.make_async_remote_copy(
            src_ref=part.at[my_rows(i), pl.ds(way * 256, 256)], dst_ref=rz2.at[way, half],
            send_sem=rs_send.at[8 + 2 * way + half], recv_sem=rz2_recv.at[2 * way + half],
            device_id=z_minus if way else z_plus, device_id_type=MESH,
        )

    def near(i, half, way):
        return pltpu.make_async_remote_copy(
            src_ref=part.at[my_rows(i), :], dst_ref=rz.at[way, half],
            send_sem=rs_send.at[12 + 2 * way + half], recv_sem=rz_recv.at[2 * way + half],
            device_id=z_minus if way else z_plus, device_id_type=MESH,
        )

    def across():
        return pltpu.make_async_remote_copy(
            src_ref=part.at[my_rows(6), :], dst_ref=ry, send_sem=rs_send.at[16], recv_sem=ry_recv.at[0],
            device_id=y_pair, device_id_type=MESH,
        )

    def handle(i):
        half = i % 2
        j = i // 2
        mine = my_rows(i)
        to_partner(i).wait_recv()
        part[mine, :] = part[mine, :] + rc[i]

        @pl.when(j == 0)
        def _():
            far(i, half, 0).start()
            far(i, half, 1).start()

        for way in range(2):
            @pl.when(j == 1 + way)
            def _():
                far(i, half, way).wait_recv()
                lanes = pl.ds(way * 256, 256)
                part[mine, lanes] = part[mine, lanes] + rz2[way, half]
                near(i, half, way).start()

    def gather_line(i, half):
        mine = my_rows(i)
        near(i, half, 0).wait_recv()
        near(i, half, 1).wait_recv()
        part[mine, :] = part[mine, :] + rz[0, half] + rz[1, half]

    prepare(tile_of(0), 0)

    def tile(i, _):
        m = tile_of(i)
        slot = i % 2
        front_copy(i).wait()

        @pl.when(i < 7)
        def _():
            front_copy(i + 1).start()

        @pl.when(m >= 4)
        def _():
            half_tile(m, slot, 0)

        def ahead():
            prepare(tile_of((i + 1) % 8), (i + 1) % 2)

        def between():
            @pl.when(i > 0)
            def _():
                handle(i - 1)

            @pl.when(i == 7)
            def _():
                gather_line(6, 0)
                across().start()

        half_tile(m, slot, 1, ahead, between)
        to_partner(i).start()
        return 0

    lax.fori_loop(0, 8, tile, 0)

    side = col % 2

    def leaf_block(k):
        return schur.at[pl.ds(at_least((side * 8 + k) * LEAF, LEAF), LEAF), pl.ds(k * LEAF, LEAF)]

    def leaf_copy(k):
        return pltpu.make_async_remote_copy(
            src_ref=leaf_block(k), dst_ref=leaf, send_sem=leaf_send.at[k], recv_sem=leaf_recv.at[0],
            device_id=(row, side * 8 + k), device_id_type=MESH,
        )

    for k in range(8):
        @pl.when((col // 2 == row) & (side * 8 + k != col))
        def _():
            leaf_copy(k).start()

        @pl.when((col // 2 == row) & (side * 8 + k == col))
        def _():
            pltpu.make_async_copy(leaf_block(k), leaf, local.at[4]).start()

    handle(7)
    gather_line(7, 1)
    across().wait_recv()
    mine = my_rows(7)
    samples = part[mine, :] + ry[...]
    off[...] = samples
    x_sends, s_sends, t_sends, f_sends = (Sends(send_sems.at[2 + i]) for i in range(4))
    x_sends.start(off, sx, g_recv.at[0], partner)

    uh[:128, :512], ul[:128, :512] = split(samples)
    arrived(sx, g_recv.at[0])
    uh[128:, :512], ul[128:, :512] = split(sx[...])
    for t in range(5):
        i = (1 - core) * (t // 4) + core * (1 + t // 2)
        j = (1 - core) * (t % 4 + t // 4) + core * (2 + t % 2 + t // 4)
        left, right = pl.ds(at_least(i * 128, 128), 128), pl.ds(at_least(j * 128, 128), 128)
        gl[t * 128 : (t + 1) * 128, :] = (
            dot_tn(uh[:, left], uh[:, right]) + dot_tn(ul[:, left], uh[:, right]) + dot_tn(uh[:, left], ul[:, right])
        )

    def chip(q):
        yy, zz = plane(q)
        return yy * 4 + zz, (x * 2 + yy // 2, (yy % 2) * 8 + zz * 2 + core)

    def share(side, q):
        return gf.at[pl.ds(at_least(side * 640 + chip(q)[0] * 40, 8), 40), :]

    for q in range(1, 16):
        index, device = chip(q)
        s_sends.start(gl.at[pl.ds(at_least(index * 40, 8), 40), :], ga.at[q], g_recv.at[1], device)
    own = chip(0)[0]
    total = gl[pl.ds(at_least(own * 40, 8), 40), :]
    arrived(ga.at[pl.ds(1, 15)], g_recv.at[1])
    for q in range(1, 16):
        total = total + ga[q]
    gf[pl.ds(at_least(core * 640 + own * 40, 8), 40), :] = total * (1.0 / 4096)
    for q in range(1, 16):
        t_sends.start(share(core, 0), share(core, 0), g_recv.at[2 + q], chip(q)[1])
    f_sends.start(share(core, 0), share(core, 0), g_recv.at[2], partner)
    for q in range(1, 16):
        back = (4 - q // 4) % 4 * 4 + (4 - q % 4) % 4
        arrived(share(core, back), g_recv.at[2 + q])
        f_sends.start(share(core, back), share(core, back), g_recv.at[2], partner)
    arrived(ga, g_recv.at[2])
    blocks = ((0, 0), (0, 1), (0, 2), (0, 3), (1, 1), (1, 2), (1, 3), (2, 2), (2, 3), (3, 3))
    for b, (i, j) in enumerate(blocks):
        block = gf[b * 128 : (b + 1) * 128, :]
        gram[i * 128 : (i + 1) * 128, j * 128 : (j + 1) * 128] = block
        if i != j:
            gram[j * 128 : (j + 1) * 128, i * 128 : (i + 1) * 128] = block.T

    holder = row * 2 + col // 8

    @pl.when(holder != col)
    def _():
        leaf_copy(0).wait_recv()

    @pl.when(holder == col)
    def _():
        pltpu.make_async_copy(leaf_block(0), leaf, local.at[4]).wait()

    for k in range(8):
        @pl.when((col // 2 == row) & (side * 8 + k != col))
        def _():
            leaf_copy(k).wait_send()

    for i in range(8):
        to_partner(i).wait_send()
    for half in range(2):
        for way in range(2):
            far(half, half, way).wait_send()
            near(2 + 2 * way + half, half, way).wait_send()
    across().wait_send()
    assert (p_sends.count, u_sends.count) == (60, 28)
    p_sends.finish(pt.at[pl.ds(0, 960), :])
    u_sends.finish(ug.at[pl.ds(0, 896), :])
    x_sends.finish(off)
    s_sends.finish(ga.at[pl.ds(1, 15)])
    t_sends.finish(ga.at[pl.ds(1, 15)])
    f_sends.finish(ga)


def emit(*refs):
    copies = [pltpu.make_async_copy(refs[i], refs[4 + i], refs[8].at[i]) for i in range(4)]
    for copy in copies:
        copy.start()
    for copy in copies:
        copy.wait()


def body(front_trailing, panel_columns, panel_rows, pivots, diag_inverse, test_matrix):
    hbm = pl.BlockSpec(memory_space=pltpu.HBM)
    vmem, dma = pltpu.VMEM, pltpu.SemaphoreType.DMA
    schur, off, leaf, gram = pl.pallas_call(
        kernel,
        out_shape=(
            pltpu.VMEM((2048, 1024), F32),
            pltpu.VMEM((128, 512), F32),
            pltpu.VMEM((128, 128), F32),
            pltpu.VMEM((512, 512), F32),
        ),
        in_specs=[hbm, hbm, hbm, pl.BlockSpec(memory_space=pltpu.VMEM), hbm, hbm],
        out_specs=(pl.BlockSpec(memory_space=pltpu.VMEM),) * 4,
        scratch_shapes=[
            vmem((1024, 2048), F32),
            vmem((1024, 1024), F32),
            vmem((1024, 1024), BF16),
            vmem((1024, 1024), BF16),
            vmem((1024, 1024), F32),
            vmem((1024, 1024), BF16),
            vmem((1024, 1024), BF16),
            vmem((TILE, 1024), BF16),
            vmem((TILE, 1024), BF16),
            vmem((2, TILE, 1024), BF16),
            vmem((2, TILE, 1024), BF16),
            vmem((2, TILE, 1024), F32),
            vmem((1024, 512), BF16),
            vmem((1024, 512), BF16),
            vmem((2048, 512), F32),
            vmem((8, 128, 512), F32),
            vmem((2, 2, 128, 256), F32),
            vmem((2, 2, 128, 512), F32),
            vmem((128, 512), F32),
            vmem((128, 512), F32),
            vmem((640, 128), F32),
            vmem((16, 40, 128), F32),
            vmem((1280, 128), F32),
            dma((6,)),
            dma((7 * PIECES,)),
            dma((2,)),
            dma((7 * PIECES,)),
            dma((17,)),
            dma((8,)),
            dma((4,)),
            dma((4,)),
            dma((1,)),
            dma((18,)),
            dma((8,)),
            dma((1,)),
            dma((5,)),
            dma((2,)),
        ],
        compiler_params=pltpu.CompilerParams(
            collective_id=0, has_side_effects=True, vmem_limit_bytes=49_000_000
        ),
        name="front",
    )(*[pltpu.with_memory_space_constraint(a, pltpu.HBM) for a in (front_trailing, panel_columns.T, panel_rows)],
      pivots.reshape(1, -1), *[pltpu.with_memory_space_constraint(a, pltpu.HBM) for a in (diag_inverse, test_matrix)])
    schur, off, leaf, gram = pl.pallas_call(
        emit,
        out_shape=[jax.ShapeDtypeStruct(a.shape, F32) for a in (schur, off, leaf, gram)],
        in_specs=[pl.BlockSpec(memory_space=pltpu.VMEM)] * 4,
        out_specs=[hbm] * 4,
        scratch_shapes=[dma((4,))],
        compiler_params=pltpu.CompilerParams(vmem_limit_bytes=2_000_000),
        name="emit",
    )(schur, off, leaf, gram)
    return schur, off, leaf, gram[None]


def solution(mesh):
    placed = (P("row", "col"), P("row", "col"), P("row", "col"), P(), P(), P("col", None))
    return jax.shard_map(
        body,
        mesh=mesh,
        in_specs=placed,
        out_specs=(
            P("row", "col"),
            P(("row", "col"), None),
            P(("row", "col"), None),
            P("row", None, None),
        ),
        check_vma=False,
    )
```

```python
import functools

import jax
import jax.numpy as jnp
from jax import lax
from jax.experimental import pallas as pl
from jax.experimental.pallas import tpu as pltpu
from jax.sharding import PartitionSpec as P

LEAF = 128
F32 = jnp.float32
BF16 = jnp.bfloat16
MESH = pl.DeviceIdType.MESH
TILE = 256


def split(x):
    high = x.astype(BF16)
    return high, (x - high.astype(F32)).astype(BF16)


def dot(a, b):
    return jnp.dot(a, b, preferred_element_type=F32)


def dot_nt(a, b):
    return lax.dot_general(a, b, (((1,), (1,)), ((), ())), preferred_element_type=F32)


def dot_tn(a, b):
    return lax.dot_general(a, b, (((0,), (0,)), ((), ())), preferred_element_type=F32)


def at_least(x, k):
    return pl.multiple_of(x, k)


class Sends:
    def __init__(self, sem):
        self.sem, self.count = sem, 0

    def start(self, src, dst, recv, device):
        self.count += 1
        pltpu.make_async_remote_copy(
            src_ref=src, dst_ref=dst, send_sem=self.sem, recv_sem=recv, device_id=device, device_id_type=MESH
        ).start()

    def finish(self, whole):
        pltpu.make_async_copy(whole, whole, self.sem).wait()


def arrived(dst, recv):
    pltpu.make_async_copy(dst, dst, recv).wait()


PIECES = 4


class Gather:
    def __init__(self, sends, recv, source, place, plus, minus, pair):
        self.sends, self.recv, self.source, self.place = sends, recv, source, place
        self.plus, self.minus, self.pair = plus, minus, pair

    def to_pair(self, piece):
        self.sends.start(self.source(piece), self.place(0, 0, piece), self.recv.at[piece], self.pair)

    def own(self, piece):
        src, dst = self.source(piece), self.place(0, 0, piece)
        self.sends.start(src, dst, self.recv.at[PIECES + piece], self.plus)
        self.sends.start(src, dst, self.recv.at[2 * PIECES + piece], self.minus)

    def where(self, slot):
        return {0: 0, 1: -1, 2: 1, 3: 2, 4: -1, 5: 1, 6: 2, 7: 0}[slot], int(slot in (0, 4, 5, 6))

    def wait(self, slot, *pieces):
        ring, pair = self.where(slot)
        for piece in pieces:
            arrived(self.place(ring, pair, piece), self.recv.at[PIECES * slot + piece])

    def spread(self, piece, up=True, down=True):
        ref = self.place(0, 1, piece)
        if up:
            self.sends.start(ref, ref, self.recv.at[4 * PIECES + piece], self.plus)
        if down:
            self.sends.start(ref, ref, self.recv.at[5 * PIECES + piece], self.minus)

    def relay(self, pair, piece):
        ring, device = (1, self.minus) if piece % 2 else (-1, self.plus)
        self.wait((1 if ring < 0 else 2) + 3 * pair, piece)
        ref = self.place(ring, pair, piece)
        self.sends.start(ref, ref, self.recv.at[PIECES * (6 if pair else 3) + piece], device)


def kernel(
    front_hbm, pt_hbm, u_hbm, piv_ref, diag_hbm, test_hbm,
    schur, off, leaf, gram,
    pt, ug, dhi, dlo, wacc, whi, wlo, uh, ul, ph, pl_, fr, thi, tlo, part,
    rc, rz2, rz, ry, sx, gl, ga, gf,
    send_sems, p_recv, core_recv, u_recv, rs_send, rc_recv, rz2_recv, rz_recv, ry_recv,
    g_recv, leaf_send, leaf_recv, local, front_sem,
):
    row, col = lax.axis_index("row"), lax.axis_index("col")
    x, yh = row // 2, row % 2
    yl, z, core = col // 8, (col % 8) // 2, col % 2
    y = yh * 2 + yl

    def p_col(dz, dy):
        return ((yl + dy) % 2) * 8 + ((z + dz + 4) % 4) * 2 + core

    def u_row(dx, dy):
        return ((x + dx + 4) % 4) * 2 + (yh + dy) % 2

    def plane(q):
        yy, zz = (y + q // 4) % 4, (z + q % 4) % 4
        return yy, zz

    partner = (row, col + 1 - 2 * core)
    z_plus, z_minus = (row, p_col(1, 0)), (row, p_col(-1, 0))
    y_pair = (row, p_col(0, 1))
    x_plus, x_minus = (u_row(1, 0), col), (u_row(-1, 0), col)
    h_pair = (u_row(0, 1), col)

    own_p = at_least(col * 64, 64)
    own_u = at_least(yh * 512 + x * 128, 128)
    loads = [
        (diag_hbm, wacc, 0),
        (u_hbm, ug.at[pl.ds(own_u, 128), :], 1),
        (test_hbm, part.at[pl.ds(0, 1024), :], 2),
        (pt_hbm, pt.at[pl.ds(own_p, 64), :], 3),
    ]
    loads = [pltpu.make_async_copy(src, dst, local.at[i]) for src, dst, i in loads]
    for copy in loads:
        copy.start()

    barrier = pltpu.get_barrier_semaphore()
    peers = [x_plus, x_minus, h_pair, y_pair, z_plus, z_minus, partner]
    for peer in peers:
        pl.semaphore_signal(barrier, inc=1, device_id=peer, device_id_type=MESH)
    pl.semaphore_wait(barrier, len(peers))

    p_sends, u_sends = Sends(send_sems.at[0]), Sends(send_sems.at[1])

    def p_place(dz, dy, piece):
        return pt.at[pl.ds(at_least(p_col(dz, dy) * 64, 64), 64), pl.ds(piece * 512, 512)]

    def u_place(dx, dy, piece):
        rows = pl.ds(at_least(((yh + dy) % 2) * 512 + ((x + dx + 4) % 4) * 128, 128), 128)
        return ug.at[rows, pl.ds(piece * 256, 256)]

    pg = Gather(p_sends, p_recv, lambda i: pt_hbm.at[:, pl.ds(i * 512, 512)], p_place, z_plus, z_minus, y_pair)
    us = Gather(u_sends, u_recv, lambda i: u_hbm.at[:, pl.ds(i * 256, 256)], u_place, x_plus, x_minus, h_pair)
    both = (pg, us)
    for piece in range(PIECES):
        for g in both:
            g.to_pair(piece)
    for piece in range(2):
        for g in both:
            g.own(piece)
    for piece in range(PIECES):
        p_sends.start(pg.source(piece), p_place(0, 0, piece), core_recv.at[piece // 2], partner)

    def hand(slot, *pieces):
        ring, pair = pg.where(slot)
        for piece in pieces:
            ref = p_place(ring, pair, piece)
            p_sends.start(ref, ref, core_recv.at[piece // 2], partner)

    def tile_of(i):
        half = i % 2
        j = i // 2
        off = 2 - j + 3 * (j // 2) - 2 * (j // 3)
        return ((yl + 1 - half) % 2) * 4 + (z + off) % 4

    def front_copy(i):
        rows = pl.ds(at_least(tile_of(i) * TILE, TILE), TILE)
        return pltpu.make_async_copy(front_hbm.at[rows, :], fr.at[i % 2], front_sem.at[i % 2])

    def early_front(m):
        lanes = pl.ds(0, 512)
        return pltpu.make_async_copy(
            front_hbm.at[pl.ds(m * TILE, TILE), lanes], fr.at[m % 2, :, lanes], front_sem.at[m % 2]
        )

    early_front(0).start()
    early_front(1).start()

    def one_hot(i, _):
        rows = pl.ds(at_least(i * TILE, TILE), TILE)
        k = lax.broadcasted_iota(jnp.int32, (TILE, 1024), 0)
        ids = (i % 2) * 512 + (i // 2) * 128 + k + (k // 128) * 128
        whi[rows, :] = jnp.where(ids == piv_ref[...], 1.0, 0.0).astype(BF16)
        return 0

    lax.fori_loop(0, 4, one_hot, 0)
    loads[0].wait()

    def permute(i, _):
        rows = pl.ds(at_least(i * TILE, TILE), TILE)
        high, low = split(wacc[rows, :])
        dhi[rows, :] = dot_nt(high, whi[...]).astype(BF16)
        dlo[rows, :] = dot_nt(low, whi[...]).astype(BF16)
        return 0

    lax.fori_loop(0, 2, permute, 0)
    for g in both:
        g.relay(0, 0)
        g.relay(0, 1)
    for g in both:
        g.wait(0, 0)
        g.spread(0)
        g.own(2)
    lax.fori_loop(2, 4, permute, 0)
    for copy in loads[1:]:
        copy.wait()

    def split_test(i, _):
        rows = pl.ds(at_least(i * TILE, TILE), TILE)
        high, low = split(part[rows, :])
        thi[rows, :] = high
        tlo[rows, :] = low
        return 0

    lax.fori_loop(0, 4, split_test, 0)

    def weight(line, pair, half, first=False, last=False):
        start = at_least(line * 512 + pair * TILE, TILE)
        lanes = slice(half * 512, half * 512 + 512)
        uh[:, :512], ul[:, :512] = split(ug[pl.ds(start, TILE), lanes])

        def step(i, _):
            rows = pl.ds(at_least(i * TILE, TILE), TILE)
            dh, dl = dhi[rows, pl.ds(start, TILE)], dlo[rows, pl.ds(start, TILE)]
            total = dot(dh, uh[:, :512]) + dot(dl, uh[:, :512]) + dot(dh, ul[:, :512])
            if not first:
                total = total + wacc[rows, lanes]
            if last:
                whi[rows, lanes], wlo[rows, lanes] = split(total)
            else:
                wacc[rows, lanes] = total
            return 0

        lax.fori_loop(0, 4, step, 0, unroll=True)

    def from_partner(which):
        arrived(pt.at[pl.ds(0, 256), :], core_recv.at[which])

    def prepare(m, slot):
        rows = pl.ds(at_least(m * TILE, TILE), TILE)
        ph[slot], pl_[slot] = split(pt[:, rows].T)

    def half_tile(m, slot, half, ahead=None, between=None):
        rows = pl.ds(at_least(m * TILE, TILE), TILE)
        lanes = slice(half * 512, half * 512 + 512)
        high = ph[slot]
        update = dot(high, whi[:, lanes]) + dot(pl_[slot], whi[:, lanes]) + dot(high, wlo[:, lanes])
        if ahead is not None:
            ahead()
        s = fr[slot, :, lanes] - update
        schur[rows, lanes] = s
        row_leaf = row * 16 + m * 2 + lax.broadcasted_iota(jnp.int32, (TILE, 512), 0) // LEAF
        col_leaf = col * 8 + half * 4 + lax.broadcasted_iota(jnp.int32, (TILE, 512), 1) // LEAF
        high, low = split(jnp.where(row_leaf == col_leaf, 0.0, s))
        if between is not None:
            between()
        samples = dot(high, thi[lanes, :]) + dot(low, thi[lanes, :]) + dot(high, tlo[lanes, :])
        part[rows, :] = part[rows, :] + samples if half else samples

    def early(m):
        early_front(m).wait()
        if m == 0:
            prepare(0, 0)
        half_tile(m, m % 2, 0, None if m == 3 else lambda: prepare(m + 1, (m + 1) % 2))
        if m < 2:
            early_front(m + 2).start()

    pg.wait(1, 1)
    pg.wait(2, 0)
    hand(1, 0, 1)
    hand(2, 0, 1)
    hand(0, 0)
    us.wait(1, 1)
    us.wait(2, 0)
    pg.wait(3, 0, 1)
    hand(3, 0, 1)
    us.wait(3, 0, 1)
    for g in both:
        g.wait(0, 1)
        g.spread(1)
    hand(0, 1)
    weight(yh, 0, 0, first=True)
    for g in both:
        g.relay(1, 0)
        g.own(3)
    hand(4, 0)
    weight(yh, 1, 0)
    for g in both:
        g.relay(1, 1)
        g.relay(0, 2)
        g.wait(0, 2)
        g.spread(2)
    pg.wait(5, 0)
    pg.wait(4, 1)
    hand(5, 0, 1)
    hand(4, 1)
    us.wait(5, 0)
    us.wait(4, 1)
    weight(1 - yh, x // 2, 0)
    for g in both:
        g.relay(0, 3)
    hand(0, 2)
    pg.wait(6, 0, 1)
    hand(6, 0, 1)
    us.wait(6, 0, 1)
    weight(1 - yh, 1 - x // 2, 0, last=True)
    from_partner(0)
    early(0)
    for g in both:
        g.wait(0, 3)
        g.spread(3)
    hand(0, 3)
    pg.wait(1, 3)
    pg.wait(2, 2)
    hand(1, 2, 3)
    hand(2, 2, 3)
    us.wait(1, 3)
    us.wait(2, 2)
    early(1)
    for g in both:
        g.relay(1, 2)
    hand(4, 2)
    pg.wait(3, 2, 3)
    hand(3, 2, 3)
    us.wait(3, 2, 3)
    early(2)
    weight(yh, 0, 1, first=True)
    for g in both:
        g.relay(1, 3)
    hand(5, 3)
    early(3)
    front_copy(0).start()
    weight(yh, 1, 1)
    pg.wait(4, 3)
    pg.wait(5, 2)
    hand(4, 3)
    hand(5, 2)
    us.wait(4, 3)
    us.wait(5, 2)
    weight(1 - yh, x // 2, 1)
    pg.wait(6, 2, 3)
    hand(6, 2, 3)
    us.wait(6, 2, 3)
    weight(1 - yh, 1 - x // 2, 1, last=True)
    from_partner(1)

    def my_rows(i):
        return pl.ds(at_least(tile_of(i) * TILE + core * 128, 128), 128)

    def its_rows(i):
        return pl.ds(at_least(tile_of(i) * TILE + 128 - core * 128, 128), 128)

    def to_partner(i):
        return pltpu.make_async_remote_copy(
            src_ref=part.at[its_rows(i), :], dst_ref=rc.at[i], send_sem=rs_send.at[i], recv_sem=rc_recv.at[i],
            device_id=partner, device_id_type=MESH,
        )

    def far(i, half, way):
        return pltpu.make_async_remote_copy(
            src_ref=part.at[my_rows(i), pl.ds(way * 256, 256)], dst_ref=rz2.at[way, half],
            send_sem=rs_send.at[8 + 2 * way + half], recv_sem=rz2_recv.at[2 * way + half],
            device_id=z_minus if way else z_plus, device_id_type=MESH,
        )

    def near(i, half, way):
        return pltpu.make_async_remote_copy(
            src_ref=part.at[my_rows(i), :], dst_ref=rz.at[way, half],
            send_sem=rs_send.at[12 + 2 * way + half], recv_sem=rz_recv.at[2 * way + half],
            device_id=z_minus if way else z_plus, device_id_type=MESH,
        )

    def across():
        return pltpu.make_async_remote_copy(
            src_ref=part.at[my_rows(6), :], dst_ref=ry, send_sem=rs_send.at[16], recv_sem=ry_recv.at[0],
            device_id=y_pair, device_id_type=MESH,
        )

    def handle(i):
        half = i % 2
        j = i // 2
        mine = my_rows(i)
        to_partner(i).wait_recv()
        part[mine, :] = part[mine, :] + rc[i]

        @pl.when(j == 0)
        def _():
            far(i, half, 0).start()
            far(i, half, 1).start()

        for way in range(2):
            @pl.when(j == 1 + way)
            def _():
                far(i, half, way).wait_recv()
                lanes = pl.ds(way * 256, 256)
                part[mine, lanes] = part[mine, lanes] + rz2[way, half]
                near(i, half, way).start()

    def gather_line(i, half):
        mine = my_rows(i)
        near(i, half, 0).wait_recv()
        near(i, half, 1).wait_recv()
        part[mine, :] = part[mine, :] + rz[0, half] + rz[1, half]

    prepare(tile_of(0), 0)

    def tile(i, _):
        m = tile_of(i)
        slot = i % 2
        front_copy(i).wait()

        @pl.when(i < 7)
        def _():
            front_copy(i + 1).start()

        @pl.when(m >= 4)
        def _():
            half_tile(m, slot, 0)

        def ahead():
            prepare(tile_of((i + 1) % 8), (i + 1) % 2)

        def between():
            @pl.when(i > 0)
            def _():
                handle(i - 1)

            @pl.when(i == 7)
            def _():
                gather_line(6, 0)
                across().start()

        half_tile(m, slot, 1, ahead, between)
        to_partner(i).start()
        return 0

    lax.fori_loop(0, 8, tile, 0)

    side = col % 2

    def leaf_block(k):
        return schur.at[pl.ds(at_least((side * 8 + k) * LEAF, LEAF), LEAF), pl.ds(k * LEAF, LEAF)]

    def leaf_copy(k):
        return pltpu.make_async_remote_copy(
            src_ref=leaf_block(k), dst_ref=leaf, send_sem=leaf_send.at[k], recv_sem=leaf_recv.at[0],
            device_id=(row, side * 8 + k), device_id_type=MESH,
        )

    for k in range(8):
        @pl.when((col // 2 == row) & (side * 8 + k != col))
        def _():
            leaf_copy(k).start()

        @pl.when((col // 2 == row) & (side * 8 + k == col))
        def _():
            pltpu.make_async_copy(leaf_block(k), leaf, local.at[4]).start()

    handle(7)
    gather_line(7, 1)
    across().wait_recv()
    mine = my_rows(7)
    samples = part[mine, :] + ry[...]
    off[...] = samples
    x_sends, s_sends, t_sends, f_sends = (Sends(send_sems.at[2 + i]) for i in range(4))
    x_sends.start(off, sx, g_recv.at[0], partner)

    uh[:128, :512], ul[:128, :512] = split(samples)
    arrived(sx, g_recv.at[0])
    uh[128:, :512], ul[128:, :512] = split(sx[...])
    for t in range(5):
        i = (1 - core) * (t // 4) + core * (1 + t // 2)
        j = (1 - core) * (t % 4 + t // 4) + core * (2 + t % 2 + t // 4)
        left, right = pl.ds(at_least(i * 128, 128), 128), pl.ds(at_least(j * 128, 128), 128)
        gl[t * 128 : (t + 1) * 128, :] = (
            dot_tn(uh[:, left], uh[:, right]) + dot_tn(ul[:, left], uh[:, right]) + dot_tn(uh[:, left], ul[:, right])
        )

    def chip(q):
        yy, zz = plane(q)
        return yy * 4 + zz, (x * 2 + yy // 2, (yy % 2) * 8 + zz * 2 + core)

    def share(side, q):
        return gf.at[pl.ds(at_least(side * 640 + chip(q)[0] * 40, 8), 40), :]

    for q in range(1, 16):
        index, device = chip(q)
        s_sends.start(gl.at[pl.ds(at_least(index * 40, 8), 40), :], ga.at[q], g_recv.at[1], device)
    own = chip(0)[0]
    total = gl[pl.ds(at_least(own * 40, 8), 40), :]
    arrived(ga.at[pl.ds(1, 15)], g_recv.at[1])
    for q in range(1, 16):
        total = total + ga[q]
    gf[pl.ds(at_least(core * 640 + own * 40, 8), 40), :] = total * (1.0 / 4096)
    for q in range(1, 16):
        t_sends.start(share(core, 0), share(core, 0), g_recv.at[2 + q], chip(q)[1])
    f_sends.start(share(core, 0), share(core, 0), g_recv.at[2], partner)
    for q in range(1, 16):
        back = (4 - q // 4) % 4 * 4 + (4 - q % 4) % 4
        arrived(share(core, back), g_recv.at[2 + q])
        f_sends.start(share(core, back), share(core, back), g_recv.at[2], partner)
    arrived(ga, g_recv.at[2])
    blocks = ((0, 0), (0, 1), (0, 2), (0, 3), (1, 1), (1, 2), (1, 3), (2, 2), (2, 3), (3, 3))
    for b, (i, j) in enumerate(blocks):
        block = gf[b * 128 : (b + 1) * 128, :]
        gram[i * 128 : (i + 1) * 128, j * 128 : (j + 1) * 128] = block
        if i != j:
            gram[j * 128 : (j + 1) * 128, i * 128 : (i + 1) * 128] = block.T

    holder = row * 2 + col // 8

    @pl.when(holder != col)
    def _():
        leaf_copy(0).wait_recv()

    @pl.when(holder == col)
    def _():
        pltpu.make_async_copy(leaf_block(0), leaf, local.at[4]).wait()

    for k in range(8):
        @pl.when((col // 2 == row) & (side * 8 + k != col))
        def _():
            leaf_copy(k).wait_send()

    for i in range(8):
        to_partner(i).wait_send()
    for half in range(2):
        for way in range(2):
            far(half, half, way).wait_send()
            near(2 + 2 * way + half, half, way).wait_send()
    across().wait_send()
    assert (p_sends.count, u_sends.count) == (60, 28)
    p_sends.finish(pt.at[pl.ds(0, 960), :])
    u_sends.finish(ug.at[pl.ds(0, 896), :])
    x_sends.finish(off)
    s_sends.finish(ga.at[pl.ds(1, 15)])
    t_sends.finish(ga.at[pl.ds(1, 15)])
    f_sends.finish(ga)


def emit(schur, off, leaf, gram, schur_out, off_out, leaf_out, gram_out, sems):
    pairs = [(schur.at[pl.ds(i * 512, 512), :], schur_out.at[pl.ds(i * 512, 512), :]) for i in range(4)]
    pairs += [(gram, gram_out), (off, off_out), (leaf, leaf_out)]
    copies = [pltpu.make_async_copy(src, dst, sems.at[i]) for i, (src, dst) in enumerate(pairs)]
    for copy in copies:
        copy.start()
    for copy in copies:
        copy.wait()


def body(front_trailing, panel_columns, panel_rows, pivots, diag_inverse, test_matrix):
    hbm = pl.BlockSpec(memory_space=pltpu.HBM)
    vmem, dma = pltpu.VMEM, pltpu.SemaphoreType.DMA
    schur, off, leaf, gram = pl.pallas_call(
        kernel,
        out_shape=(
            pltpu.VMEM((2048, 1024), F32),
            pltpu.VMEM((128, 512), F32),
            pltpu.VMEM((128, 128), F32),
            pltpu.VMEM((512, 512), F32),
        ),
        in_specs=[hbm, hbm, hbm, pl.BlockSpec(memory_space=pltpu.VMEM), hbm, hbm],
        out_specs=(pl.BlockSpec(memory_space=pltpu.VMEM),) * 4,
        scratch_shapes=[
            vmem((1024, 2048), F32),
            vmem((1024, 1024), F32),
            vmem((1024, 1024), BF16),
            vmem((1024, 1024), BF16),
            vmem((1024, 1024), F32),
            vmem((1024, 1024), BF16),
            vmem((1024, 1024), BF16),
            vmem((TILE, 1024), BF16),
            vmem((TILE, 1024), BF16),
            vmem((2, TILE, 1024), BF16),
            vmem((2, TILE, 1024), BF16),
            vmem((2, TILE, 1024), F32),
            vmem((1024, 512), BF16),
            vmem((1024, 512), BF16),
            vmem((2048, 512), F32),
            vmem((8, 128, 512), F32),
            vmem((2, 2, 128, 256), F32),
            vmem((2, 2, 128, 512), F32),
            vmem((128, 512), F32),
            vmem((128, 512), F32),
            vmem((640, 128), F32),
            vmem((16, 40, 128), F32),
            vmem((1280, 128), F32),
            dma((6,)),
            dma((7 * PIECES,)),
            dma((2,)),
            dma((7 * PIECES,)),
            dma((17,)),
            dma((8,)),
            dma((4,)),
            dma((4,)),
            dma((1,)),
            dma((18,)),
            dma((8,)),
            dma((1,)),
            dma((5,)),
            dma((2,)),
        ],
        compiler_params=pltpu.CompilerParams(
            collective_id=0, has_side_effects=True, vmem_limit_bytes=49_000_000
        ),
        name="front",
    )(*[pltpu.with_memory_space_constraint(a, pltpu.HBM) for a in (front_trailing, panel_columns.T, panel_rows)],
      pivots.reshape(1, -1), *[pltpu.with_memory_space_constraint(a, pltpu.HBM) for a in (diag_inverse, test_matrix)])
    schur, off, leaf, gram = pl.pallas_call(
        emit,
        out_shape=[jax.ShapeDtypeStruct(a.shape, F32) for a in (schur, off, leaf, gram)],
        in_specs=[pl.BlockSpec(memory_space=pltpu.VMEM)] * 4,
        out_specs=[hbm] * 4,
        scratch_shapes=[dma((7,))],
        compiler_params=pltpu.CompilerParams(vmem_limit_bytes=2_000_000),
        name="emit",
    )(schur, off, leaf, gram)
    return schur, off, leaf, gram[None]


def solution(mesh):
    placed = (P("row", "col"), P("row", "col"), P("row", "col"), P(), P(), P("col", None))
    return jax.shard_map(
        body,
        mesh=mesh,
        in_specs=placed,
        out_specs=(
            P("row", "col"),
            P(("row", "col"), None),
            P(("row", "col"), None),
            P("row", None, None),
        ),
        check_vma=False,
    )
```

```python
import functools

import jax
import jax.numpy as jnp
from jax import lax
from jax.experimental import pallas as pl
from jax.experimental.pallas import tpu as pltpu
from jax.sharding import PartitionSpec as P

LEAF = 128
F32 = jnp.float32
BF16 = jnp.bfloat16
MESH = pl.DeviceIdType.MESH
TILE = 256


def split(x):
    high = x.astype(BF16)
    return high, (x - high.astype(F32)).astype(BF16)


def dot(a, b):
    return jnp.dot(a, b, preferred_element_type=F32)


def dot_nt(a, b):
    return lax.dot_general(a, b, (((1,), (1,)), ((), ())), preferred_element_type=F32)


def dot_tn(a, b):
    return lax.dot_general(a, b, (((0,), (0,)), ((), ())), preferred_element_type=F32)


def at_least(x, k):
    return pl.multiple_of(x, k)


class Sends:
    def __init__(self, sem):
        self.sem, self.count = sem, 0

    def start(self, src, dst, recv, device):
        self.count += 1
        pltpu.make_async_remote_copy(
            src_ref=src, dst_ref=dst, send_sem=self.sem, recv_sem=recv, device_id=device, device_id_type=MESH
        ).start()

    def finish(self, whole):
        pltpu.make_async_copy(whole, whole, self.sem).wait()


def arrived(dst, recv):
    pltpu.make_async_copy(dst, dst, recv).wait()


PIECES = 4


class Gather:
    def __init__(self, sends, recv, source, place, plus, minus, pair):
        self.sends, self.recv, self.source, self.place = sends, recv, source, place
        self.plus, self.minus, self.pair = plus, minus, pair

    def to_pair(self, piece):
        self.sends.start(self.source(piece), self.place(0, 0, piece), self.recv.at[piece], self.pair)

    def own(self, piece):
        src, dst = self.source(piece), self.place(0, 0, piece)
        self.sends.start(src, dst, self.recv.at[PIECES + piece], self.plus)
        self.sends.start(src, dst, self.recv.at[2 * PIECES + piece], self.minus)

    def where(self, slot):
        return {0: 0, 1: -1, 2: 1, 3: 2, 4: -1, 5: 1, 6: 2, 7: 0}[slot], int(slot in (0, 4, 5, 6))

    def wait(self, slot, *pieces):
        ring, pair = self.where(slot)
        for piece in pieces:
            arrived(self.place(ring, pair, piece), self.recv.at[PIECES * slot + piece])

    def spread(self, piece, up=True, down=True):
        ref = self.place(0, 1, piece)
        if up:
            self.sends.start(ref, ref, self.recv.at[4 * PIECES + piece], self.plus)
        if down:
            self.sends.start(ref, ref, self.recv.at[5 * PIECES + piece], self.minus)

    def relay(self, pair, piece):
        ring, device = (1, self.minus) if piece % 2 else (-1, self.plus)
        self.wait((1 if ring < 0 else 2) + 3 * pair, piece)
        ref = self.place(ring, pair, piece)
        self.sends.start(ref, ref, self.recv.at[PIECES * (6 if pair else 3) + piece], device)


def kernel(
    front_hbm, pt_hbm, u_hbm, piv_ref, diag_hbm, test_hbm,
    schur, off, leaf, gram,
    pt, ug, dhi, dlo, wacc, whi, wlo, uh, ul, ph, pl_, fr, thi, tlo, part,
    rc, rz2, rz, ry, sx, gl, ga, gf,
    send_sems, p_recv, core_recv, u_recv, rs_send, rc_recv, rz2_recv, rz_recv, ry_recv,
    g_recv, leaf_send, leaf_recv, local, front_sem,
):
    row, col = lax.axis_index("row"), lax.axis_index("col")
    x, yh = row // 2, row % 2
    yl, z, core = col // 8, (col % 8) // 2, col % 2
    y = yh * 2 + yl

    def p_col(dz, dy):
        return ((yl + dy) % 2) * 8 + ((z + dz + 4) % 4) * 2 + core

    def u_row(dx, dy):
        return ((x + dx + 4) % 4) * 2 + (yh + dy) % 2

    def plane(q):
        yy, zz = (y + q // 4) % 4, (z + q % 4) % 4
        return yy, zz

    partner = (row, col + 1 - 2 * core)
    z_plus, z_minus = (row, p_col(1, 0)), (row, p_col(-1, 0))
    y_pair = (row, p_col(0, 1))
    x_plus, x_minus = (u_row(1, 0), col), (u_row(-1, 0), col)
    h_pair = (u_row(0, 1), col)

    own_p = at_least(col * 64, 64)
    own_u = at_least(yh * 512 + x * 128, 128)
    loads = [
        (diag_hbm, wacc, 0),
        (u_hbm, ug.at[pl.ds(own_u, 128), :], 1),
        (test_hbm, part.at[pl.ds(0, 1024), :], 2),
        (pt_hbm, pt.at[pl.ds(own_p, 64), :], 3),
    ]
    loads = [pltpu.make_async_copy(src, dst, local.at[i]) for src, dst, i in loads]
    for copy in loads:
        copy.start()

    barrier = pltpu.get_barrier_semaphore()
    peers = [x_plus, x_minus, h_pair, y_pair, z_plus, z_minus, partner]
    for peer in peers:
        pl.semaphore_signal(barrier, inc=1, device_id=peer, device_id_type=MESH)
    pl.semaphore_wait(barrier, len(peers))

    p_sends, u_sends = Sends(send_sems.at[0]), Sends(send_sems.at[1])

    def p_place(dz, dy, piece):
        return pt.at[pl.ds(at_least(p_col(dz, dy) * 64, 64), 64), pl.ds(piece * 512, 512)]

    def u_place(dx, dy, piece):
        rows = pl.ds(at_least(((yh + dy) % 2) * 512 + ((x + dx + 4) % 4) * 128, 128), 128)
        return ug.at[rows, pl.ds(piece * 256, 256)]

    pg = Gather(p_sends, p_recv, lambda i: pt_hbm.at[:, pl.ds(i * 512, 512)], p_place, z_plus, z_minus, y_pair)
    us = Gather(u_sends, u_recv, lambda i: u_hbm.at[:, pl.ds(i * 256, 256)], u_place, x_plus, x_minus, h_pair)
    both = (pg, us)
    for piece in range(PIECES):
        for g in both:
            g.to_pair(piece)
    for piece in range(2):
        for g in both:
            g.own(piece)
    for piece in range(PIECES):
        p_sends.start(pg.source(piece), p_place(0, 0, piece), core_recv.at[piece // 2], partner)

    def hand(slot, *pieces):
        ring, pair = pg.where(slot)
        for piece in pieces:
            ref = p_place(ring, pair, piece)
            p_sends.start(ref, ref, core_recv.at[piece // 2], partner)

    def tile_of(i):
        half = i % 2
        j = i // 2
        off = 2 - j + 3 * (j // 2) - 2 * (j // 3)
        return ((yl + 1 - half) % 2) * 4 + (z + off) % 4

    def front_copy(i):
        rows = pl.ds(at_least(tile_of(i) * TILE, TILE), TILE)
        return pltpu.make_async_copy(front_hbm.at[rows, :], fr.at[i % 2], front_sem.at[i % 2])

    def early_front(m):
        lanes = pl.ds(0, 512)
        return pltpu.make_async_copy(
            front_hbm.at[pl.ds(m * TILE, TILE), lanes], fr.at[m % 2, :, lanes], front_sem.at[m % 2]
        )

    early_front(0).start()
    early_front(1).start()

    def one_hot(i, _):
        rows = pl.ds(at_least(i * TILE, TILE), TILE)
        k = lax.broadcasted_iota(jnp.int32, (TILE, 1024), 0)
        ids = (i % 2) * 512 + (i // 2) * 128 + k + (k // 128) * 128
        whi[rows, :] = jnp.where(ids == piv_ref[...], 1.0, 0.0).astype(BF16)
        return 0

    lax.fori_loop(0, 4, one_hot, 0)
    loads[0].wait()

    def permute(i, _):
        rows = pl.ds(at_least(i * TILE, TILE), TILE)
        high, low = split(wacc[rows, :])
        dhi[rows, :] = dot_nt(high, whi[...]).astype(BF16)
        dlo[rows, :] = dot_nt(low, whi[...]).astype(BF16)
        return 0

    lax.fori_loop(0, 2, permute, 0)
    for g in both:
        g.relay(0, 0)
        g.relay(0, 1)
    for g in both:
        g.own(2)
    for g in both:
        g.wait(0, 0)
        g.spread(0)
    lax.fori_loop(2, 4, permute, 0)
    for copy in loads[1:]:
        copy.wait()

    def split_test(i, _):
        rows = pl.ds(at_least(i * TILE, TILE), TILE)
        high, low = split(part[rows, :])
        thi[rows, :] = high
        tlo[rows, :] = low
        return 0

    lax.fori_loop(0, 4, split_test, 0)

    def weight(line, pair, half, first=False, last=False):
        start = at_least(line * 512 + pair * TILE, TILE)
        lanes = slice(half * 512, half * 512 + 512)
        uh[:, :512], ul[:, :512] = split(ug[pl.ds(start, TILE), lanes])

        def step(i, _):
            rows = pl.ds(at_least(i * TILE, TILE), TILE)
            dh, dl = dhi[rows, pl.ds(start, TILE)], dlo[rows, pl.ds(start, TILE)]
            total = dot(dh, uh[:, :512]) + dot(dl, uh[:, :512]) + dot(dh, ul[:, :512])
            if not first:
                total = total + wacc[rows, lanes]
            if last:
                whi[rows, lanes], wlo[rows, lanes] = split(total)
            else:
                wacc[rows, lanes] = total
            return 0

        lax.fori_loop(0, 4, step, 0, unroll=True)

    def from_partner(which):
        arrived(pt.at[pl.ds(0, 256), :], core_recv.at[which])

    def prepare(m, slot):
        rows = pl.ds(at_least(m * TILE, TILE), TILE)
        ph[slot], pl_[slot] = split(pt[:, rows].T)

    def half_tile(m, slot, half, ahead=None, between=None):
        rows = pl.ds(at_least(m * TILE, TILE), TILE)
        lanes = slice(half * 512, half * 512 + 512)
        high = ph[slot]
        update = dot(high, whi[:, lanes]) + dot(pl_[slot], whi[:, lanes]) + dot(high, wlo[:, lanes])
        if ahead is not None:
            ahead()
        s = fr[slot, :, lanes] - update
        schur[rows, lanes] = s
        row_leaf = row * 16 + m * 2 + lax.broadcasted_iota(jnp.int32, (TILE, 512), 0) // LEAF
        col_leaf = col * 8 + half * 4 + lax.broadcasted_iota(jnp.int32, (TILE, 512), 1) // LEAF
        high, low = split(jnp.where(row_leaf == col_leaf, 0.0, s))
        if between is not None:
            between()
        samples = dot(high, thi[lanes, :]) + dot(low, thi[lanes, :]) + dot(high, tlo[lanes, :])
        part[rows, :] = part[rows, :] + samples if half else samples

    def early(m):
        early_front(m).wait()
        if m == 0:
            prepare(0, 0)
        half_tile(m, m % 2, 0, None if m == 3 else lambda: prepare(m + 1, (m + 1) % 2))
        if m < 2:
            early_front(m + 2).start()

    pg.wait(1, 1)
    pg.wait(2, 0)
    hand(1, 0, 1)
    hand(2, 0, 1)
    hand(0, 0)
    us.wait(1, 1)
    us.wait(2, 0)
    pg.wait(3, 0, 1)
    hand(3, 0, 1)
    us.wait(3, 0, 1)
    for g in both:
        g.wait(0, 1)
        g.spread(1)
        g.own(3)
    hand(0, 1)
    weight(yh, 0, 0, first=True)
    for g in both:
        g.relay(1, 0)
    hand(4, 0)
    weight(yh, 1, 0)
    for g in both:
        g.relay(1, 1)
        g.relay(0, 2)
        g.wait(0, 2)
        g.spread(2)
    pg.wait(5, 0)
    pg.wait(4, 1)
    hand(5, 0, 1)
    hand(4, 1)
    us.wait(5, 0)
    us.wait(4, 1)
    weight(1 - yh, x // 2, 0)
    for g in both:
        g.relay(0, 3)
    hand(0, 2)
    pg.wait(6, 0, 1)
    hand(6, 0, 1)
    us.wait(6, 0, 1)
    weight(1 - yh, 1 - x // 2, 0, last=True)
    from_partner(0)
    early(0)
    for g in both:
        g.wait(0, 3)
        g.spread(3)
    hand(0, 3)
    pg.wait(1, 3)
    pg.wait(2, 2)
    hand(1, 2, 3)
    hand(2, 2, 3)
    us.wait(1, 3)
    us.wait(2, 2)
    early(1)
    for g in both:
        g.relay(1, 2)
    hand(4, 2)
    pg.wait(3, 2, 3)
    hand(3, 2, 3)
    us.wait(3, 2, 3)
    early(2)
    weight(yh, 0, 1, first=True)
    for g in both:
        g.relay(1, 3)
    hand(5, 3)
    early(3)
    front_copy(0).start()
    weight(yh, 1, 1)
    pg.wait(4, 3)
    pg.wait(5, 2)
    hand(4, 3)
    hand(5, 2)
    us.wait(4, 3)
    us.wait(5, 2)
    weight(1 - yh, x // 2, 1)
    pg.wait(6, 2, 3)
    hand(6, 2, 3)
    us.wait(6, 2, 3)
    weight(1 - yh, 1 - x // 2, 1, last=True)
    from_partner(1)

    def my_rows(i):
        return pl.ds(at_least(tile_of(i) * TILE + core * 128, 128), 128)

    def its_rows(i):
        return pl.ds(at_least(tile_of(i) * TILE + 128 - core * 128, 128), 128)

    def to_partner(i):
        return pltpu.make_async_remote_copy(
            src_ref=part.at[its_rows(i), :], dst_ref=rc.at[i], send_sem=rs_send.at[0], recv_sem=rc_recv.at[i],
            device_id=partner, device_id_type=MESH,
        )

    def far(i, half, way):
        return pltpu.make_async_remote_copy(
            src_ref=part.at[my_rows(i), pl.ds(way * 256, 256)], dst_ref=rz2.at[way, half],
            send_sem=rs_send.at[8 + 2 * way + half], recv_sem=rz2_recv.at[2 * way + half],
            device_id=z_minus if way else z_plus, device_id_type=MESH,
        )

    def near(i, half, way):
        return pltpu.make_async_remote_copy(
            src_ref=part.at[my_rows(i), :], dst_ref=rz.at[way, half],
            send_sem=rs_send.at[12 + 2 * way + half], recv_sem=rz_recv.at[2 * way + half],
            device_id=z_minus if way else z_plus, device_id_type=MESH,
        )

    def across():
        return pltpu.make_async_remote_copy(
            src_ref=part.at[my_rows(6), :], dst_ref=ry, send_sem=rs_send.at[16], recv_sem=ry_recv.at[0],
            device_id=y_pair, device_id_type=MESH,
        )

    def handle(i):
        half = i % 2
        j = i // 2
        mine = my_rows(i)
        to_partner(i).wait_recv()
        part[mine, :] = part[mine, :] + rc[i]

        @pl.when(j == 0)
        def _():
            far(i, half, 0).start()
            far(i, half, 1).start()

        for way in range(2):
            @pl.when(j == 1 + way)
            def _():
                far(i, half, way).wait_recv()
                lanes = pl.ds(way * 256, 256)
                part[mine, lanes] = part[mine, lanes] + rz2[way, half]
                near(i, half, way).start()

    def gather_line(i, half):
        mine = my_rows(i)
        near(i, half, 0).wait_recv()
        near(i, half, 1).wait_recv()
        part[mine, :] = part[mine, :] + rz[0, half] + rz[1, half]

    prepare(tile_of(0), 0)

    def tile(i, _):
        m = tile_of(i)
        slot = i % 2
        front_copy(i).wait()

        @pl.when(i < 7)
        def _():
            front_copy(i + 1).start()

        @pl.when(m >= 4)
        def _():
            half_tile(m, slot, 0)

        def ahead():
            prepare(tile_of((i + 1) % 8), (i + 1) % 2)

        def between():
            @pl.when(i > 0)
            def _():
                handle(i - 1)

            @pl.when(i == 7)
            def _():
                gather_line(6, 0)
                across().start()

        half_tile(m, slot, 1, ahead, between)
        to_partner(i).start()
        return 0

    lax.fori_loop(0, 8, tile, 0)

    side = col % 2

    def leaf_block(k):
        return schur.at[pl.ds(at_least((side * 8 + k) * LEAF, LEAF), LEAF), pl.ds(k * LEAF, LEAF)]

    def leaf_copy(k):
        return pltpu.make_async_remote_copy(
            src_ref=leaf_block(k), dst_ref=leaf, send_sem=leaf_send.at[k], recv_sem=leaf_recv.at[0],
            device_id=(row, side * 8 + k), device_id_type=MESH,
        )

    for k in range(8):
        @pl.when((col // 2 == row) & (side * 8 + k != col))
        def _():
            leaf_copy(k).start()

        @pl.when((col // 2 == row) & (side * 8 + k == col))
        def _():
            pltpu.make_async_copy(leaf_block(k), leaf, local.at[4]).start()

    handle(7)
    gather_line(7, 1)
    across().wait_recv()
    mine = my_rows(7)
    samples = part[mine, :] + ry[...]
    off[...] = samples
    x_sends, s_sends, t_sends, f_sends = (Sends(send_sems.at[2 + i]) for i in range(4))
    x_sends.start(off, sx, g_recv.at[0], partner)

    uh[:128, :512], ul[:128, :512] = split(samples)
    arrived(sx, g_recv.at[0])
    uh[128:, :512], ul[128:, :512] = split(sx[...])
    for t in range(5):
        i = (1 - core) * (t // 4) + core * (1 + t // 2)
        j = (1 - core) * (t % 4 + t // 4) + core * (2 + t % 2 + t // 4)
        left, right = pl.ds(at_least(i * 128, 128), 128), pl.ds(at_least(j * 128, 128), 128)
        gl[t * 128 : (t + 1) * 128, :] = (
            dot_tn(uh[:, left], uh[:, right]) + dot_tn(ul[:, left], uh[:, right]) + dot_tn(uh[:, left], ul[:, right])
        )

    def chip(q):
        yy, zz = plane(q)
        return yy * 4 + zz, (x * 2 + yy // 2, (yy % 2) * 8 + zz * 2 + core)

    def share(side, q):
        return gf.at[pl.ds(at_least(side * 640 + chip(q)[0] * 40, 8), 40), :]

    for q in range(1, 16):
        index, device = chip(q)
        s_sends.start(gl.at[pl.ds(at_least(index * 40, 8), 40), :], ga.at[q], g_recv.at[1], device)
    own = chip(0)[0]
    total = gl[pl.ds(at_least(own * 40, 8), 40), :]
    arrived(ga.at[pl.ds(1, 15)], g_recv.at[1])
    for q in range(1, 16):
        total = total + ga[q]
    gf[pl.ds(at_least(core * 640 + own * 40, 8), 40), :] = total * (1.0 / 4096)
    for q in range(1, 16):
        t_sends.start(share(core, 0), share(core, 0), g_recv.at[2 + q], chip(q)[1])
    f_sends.start(share(core, 0), share(core, 0), g_recv.at[2], partner)
    for q in range(1, 16):
        back = (4 - q // 4) % 4 * 4 + (4 - q % 4) % 4
        arrived(share(core, back), g_recv.at[2 + q])
        f_sends.start(share(core, back), share(core, back), g_recv.at[2], partner)
    arrived(ga, g_recv.at[2])
    blocks = ((0, 0), (0, 1), (0, 2), (0, 3), (1, 1), (1, 2), (1, 3), (2, 2), (2, 3), (3, 3))
    for b, (i, j) in enumerate(blocks):
        block = gf[b * 128 : (b + 1) * 128, :]
        gram[i * 128 : (i + 1) * 128, j * 128 : (j + 1) * 128] = block
        if i != j:
            gram[j * 128 : (j + 1) * 128, i * 128 : (i + 1) * 128] = block.T

    holder = row * 2 + col // 8

    @pl.when(holder != col)
    def _():
        leaf_copy(0).wait_recv()

    @pl.when(holder == col)
    def _():
        pltpu.make_async_copy(leaf_block(0), leaf, local.at[4]).wait()

    for k in range(8):
        @pl.when((col // 2 == row) & (side * 8 + k != col))
        def _():
            leaf_copy(k).wait_send()

    pltpu.make_async_copy(rc, rc, rs_send.at[0]).wait()
    for half in range(2):
        for way in range(2):
            far(half, half, way).wait_send()
            near(2 + 2 * way + half, half, way).wait_send()
    across().wait_send()
    assert (p_sends.count, u_sends.count) == (60, 28)
    p_sends.finish(pt.at[pl.ds(0, 960), :])
    u_sends.finish(ug.at[pl.ds(0, 896), :])
    x_sends.finish(off)
    s_sends.finish(ga.at[pl.ds(1, 15)])
    t_sends.finish(ga.at[pl.ds(1, 15)])
    f_sends.finish(ga)


def emit(schur, off, leaf, gram, schur_out, off_out, leaf_out, gram_out, sems):
    pairs = [(schur.at[pl.ds(i * 512, 512), :], schur_out.at[pl.ds(i * 512, 512), :]) for i in range(4)]
    pairs += [(gram, gram_out), (off, off_out), (leaf, leaf_out)]
    copies = [pltpu.make_async_copy(src, dst, sems.at[i]) for i, (src, dst) in enumerate(pairs)]
    for copy in copies:
        copy.start()
    for copy in copies:
        copy.wait()


def body(front_trailing, panel_columns, panel_rows, pivots, diag_inverse, test_matrix):
    hbm = pl.BlockSpec(memory_space=pltpu.HBM)
    vmem, dma = pltpu.VMEM, pltpu.SemaphoreType.DMA
    schur, off, leaf, gram = pl.pallas_call(
        kernel,
        out_shape=(
            pltpu.VMEM((2048, 1024), F32),
            pltpu.VMEM((128, 512), F32),
            pltpu.VMEM((128, 128), F32),
            pltpu.VMEM((512, 512), F32),
        ),
        in_specs=[hbm, hbm, hbm, pl.BlockSpec(memory_space=pltpu.VMEM), hbm, hbm],
        out_specs=(pl.BlockSpec(memory_space=pltpu.VMEM),) * 4,
        scratch_shapes=[
            vmem((1024, 2048), F32),
            vmem((1024, 1024), F32),
            vmem((1024, 1024), BF16),
            vmem((1024, 1024), BF16),
            vmem((1024, 1024), F32),
            vmem((1024, 1024), BF16),
            vmem((1024, 1024), BF16),
            vmem((TILE, 1024), BF16),
            vmem((TILE, 1024), BF16),
            vmem((2, TILE, 1024), BF16),
            vmem((2, TILE, 1024), BF16),
            vmem((2, TILE, 1024), F32),
            vmem((1024, 512), BF16),
            vmem((1024, 512), BF16),
            vmem((2048, 512), F32),
            vmem((8, 128, 512), F32),
            vmem((2, 2, 128, 256), F32),
            vmem((2, 2, 128, 512), F32),
            vmem((128, 512), F32),
            vmem((128, 512), F32),
            vmem((640, 128), F32),
            vmem((16, 40, 128), F32),
            vmem((1280, 128), F32),
            dma((6,)),
            dma((7 * PIECES,)),
            dma((2,)),
            dma((7 * PIECES,)),
            dma((17,)),
            dma((8,)),
            dma((4,)),
            dma((4,)),
            dma((1,)),
            dma((18,)),
            dma((8,)),
            dma((1,)),
            dma((5,)),
            dma((2,)),
        ],
        compiler_params=pltpu.CompilerParams(
            collective_id=0, has_side_effects=True, vmem_limit_bytes=49_000_000
        ),
        name="front",
    )(*[pltpu.with_memory_space_constraint(a, pltpu.HBM) for a in (front_trailing, panel_columns.T, panel_rows)],
      pivots.reshape(1, -1), *[pltpu.with_memory_space_constraint(a, pltpu.HBM) for a in (diag_inverse, test_matrix)])
    schur, off, leaf, gram = pl.pallas_call(
        emit,
        out_shape=[jax.ShapeDtypeStruct(a.shape, F32) for a in (schur, off, leaf, gram)],
        in_specs=[pl.BlockSpec(memory_space=pltpu.VMEM)] * 4,
        out_specs=[hbm] * 4,
        scratch_shapes=[dma((7,))],
        compiler_params=pltpu.CompilerParams(vmem_limit_bytes=2_000_000),
        name="emit",
    )(schur, off, leaf, gram)
    return schur, off, leaf, gram[None]


def solution(mesh):
    placed = (P("row", "col"), P("row", "col"), P("row", "col"), P(), P(), P("col", None))
    return jax.shard_map(
        body,
        mesh=mesh,
        in_specs=placed,
        out_specs=(
            P("row", "col"),
            P(("row", "col"), None),
            P(("row", "col"), None),
            P("row", None, None),
        ),
        check_vma=False,
    )
```
